128 devices in a mesh: wave: 16 (over y, x), atm: 8 (over z, core).
Axes of the slice: x: 4, y: 4, z: 4, core: 2. Of those that a mesh axis runs over, the one named last changes fastest.
Arguments:
- spectra: bfloat16 [1296, 262144], P(None, ('wave', 'atm')), may hold values from 0.049804688 to 2
- interact: bfloat16 [1296, 1296], replicated, may hold values from -0.15625 to 0.15625
- sea_mask: int32 [262144], P(('wave', 'atm')), may hold values 0 or 1
- sea_tile: int32 [262144], P(('wave', 'atm')), may hold values from 0 to 127, as said below
- push_list: int32 [128, 128, 32], P(('wave', 'atm')), may hold values from -1 to 8191, as said below
- neighbors: int32 [4, 262144], P(None, ('wave', 'atm')), may hold values from 0 to 3071, as said below
- air_wind: float32 [2, 512, 2048], P(None, 'atm', 'wave'), may hold values from -6 to 6
- diffusion: float32 [512, 2048], P('atm', 'wave'), may hold values from 0.04 to 0.2
Outputs:
- wave_spectra: bfloat16 [1296, 262144], P(None, ('wave', 'atm'))
- surface_wind: float32 [2, 512, 2048], P(None, 'atm', 'wave')
- roughness: float32 [512, 2048], P('atm', 'wave')
The draws below stay inside these ranges and needn't reach their ends.
Inputs may be any that keep to these rules, and one draw needn't show every extreme that they name: `sea_tile`: tile t covers atmosphere rows from (t mod 8) * 64 and columns from (t div 8) * 128. In every block no tile lies above more than 32 of its points, and in every block some tile lies above exactly 32. `push_list`: entry [t, b, r] is the cell, row-major within tile t, under the r-th sea point of block b (in point order) whose tile is t, and -1 for r at or past the number of such points. `neighbors`: entries index the block's points extended by 512 points of each adjacent block: index 512 + i is the block's point i. West and east of point i are 512 + i - 1 and 512 + i + 1; south lies from i to 512 + i, north from 512 + i to 1024 + i.
All inputs are finite; a program needn't handle non-finite values. No bound on the sum of `sea_mask` on one device may be relied on, other than what follows from the above.
Results may differ from the reference program's by a relative error of at most 0.0046.
Values may be sent and summed in bfloat16 or wider, within the bound.
No kernel may reach another device: no remote copies, remote signals or barrier semaphores. Data moves between devices by JAX's collectives and lax.ppermute only.
A program may use at most 256 MiB of HBM per device.

```python
import math
import jax
import jax.numpy as jnp
from jax import lax

ND = 36
NF = 36
K = 1296
P_DEV = 2048
H = 512
LAT_DEV = 64
LON_DEV = 128
ATM_STEPS = 4
BLOCKS = 128
NPTS = 262144
NLAT = 512
NLON = 2048
CELLS = 8192
CAP = 32
N_ATM = 8


def coupling_tables(key):
    base = jax.random.fold_in(key, 11)
    slot_total = BLOCKS * CAP

    def one_block(block):
        block_key = jax.random.fold_in(base, block)
        keys = jax.random.split(block_key, 5)
        favour = jax.random.randint(keys[0], (BLOCKS,), 0, 4)
        filled = jax.random.randint(keys[1], (), 0, BLOCKS)
        favour = jnp.where(jnp.arange(BLOCKS) == filled, 8, favour)
        noise = jax.random.randint(keys[2], (slot_total,), 0, 256)
        slot_owner = jnp.arange(slot_total, dtype=jnp.int32) // CAP
        scores = (favour[slot_owner] * 256 + noise) * slot_total + jnp.arange(slot_total, dtype=jnp.int32)
        unused, chosen = lax.top_k(scores, P_DEV)
        owners = (chosen // CAP).astype(jnp.int32)
        shuffle = jax.random.permutation(keys[3], P_DEV)
        owner_points = jnp.zeros((P_DEV,), jnp.int32).at[shuffle].set(owners)
        cells = jax.random.randint(keys[4], (P_DEV,), 0, CELLS).astype(jnp.int32)
        tile_hot = (owner_points[:, None] == jnp.arange(BLOCKS, dtype=jnp.int32)[None, :]).astype(jnp.int32)
        ranked = jnp.sum(jnp.cumsum(tile_hot, axis=0) * tile_hot, axis=1) - 1
        listing = jnp.full((BLOCKS, CAP), -1, jnp.int32).at[owner_points, ranked].set(cells)
        return (owner_points, listing)
    owners, listings = jax.vmap(one_block)(jnp.arange(BLOCKS, dtype=jnp.int32))
    return (owners.reshape(-1), jnp.transpose(listings, (1, 0, 2)))


def draw_sea_tile(key, part):
    owners, listings = coupling_tables(key)
    return owners


def draw_push_list(key, part):
    owners, listings = coupling_tables(key)
    return listings


def draw_neighbors(key, part):
    keys = jax.random.split(jax.random.fold_in(key, 23), 2)
    position = jnp.arange(NPTS, dtype=jnp.int32) % P_DEV
    jitter_south = jax.random.randint(keys[0], (NPTS,), 0, H // 4 + 1)
    jitter_north = jax.random.randint(keys[1], (NPTS,), 0, H // 4 + 1)
    jitter_south = jnp.where(position == 0, 0, jitter_south)
    jitter_north = jnp.where(position == P_DEV - 1, 0, jitter_north)
    west_side = H + position - 1
    east_side = H + position + 1
    south_side = position + jitter_south
    north_side = 2 * H + position - jitter_north
    return jnp.stack([west_side, east_side, south_side, north_side]).astype(jnp.int32)


def touch_ends(values, rng, least, largest):
    shape = values.shape
    spot = [jax.random.randint(jax.random.fold_in(rng, axis), (), 0, shape[axis]) for axis in range(len(shape))]
    values = values.at[tuple(spot)].set(least)
    longest = shape.index(max(shape))
    spot[longest] = (spot[longest] + 1) % shape[longest]
    return values.at[tuple(spot)].set(largest)


def levels(stream_key, dims, cuts, least, high):
    gain = 1.0
    for dim, blocks in cuts:
        steps = jax.random.uniform(jax.random.fold_in(jax.random.fold_in(stream_key, 6), dim), (blocks,), jnp.float32, least / len(cuts), high / len(cuts))
        gain = gain * jnp.repeat(jnp.exp(steps), dims[dim] // blocks).reshape((-1,) + (1,) * (len(dims) - 1 - dim))
    return gain


def normal_values(rng, dims, width, bound, cuts=(), held_as=jnp.bfloat16):
    factor_of = levels(rng, dims, cuts, -0.22, 0.18) if cuts else 1.0
    drawn = jax.random.normal(rng, dims, jnp.float32) * width * factor_of
    return jnp.minimum(jnp.maximum(drawn, -bound), bound).astype(held_as)


def setup_inputs(seed: int = 0) -> dict:
    key_of = jax.random.split(jax.random.key(seed), 9)
    spectra = jnp.clip(jnp.exp(math.log(2.0) - 3.6927934 * jax.random.uniform(key_of[0], (K, NPTS), jnp.float32) ** levels(key_of[0], (K, NPTS), ((1, 128),), -0.2, 0.2)), 0.049804688, 2.0).astype(jnp.bfloat16)
    interact = normal_values(key_of[1], (K, K), K ** -0.5, 0.15625)
    sea_mask = touch_ends((jax.random.randint(key_of[2], (NPTS,), 0, 4) < 3).astype(jnp.int32), jax.random.fold_in(key_of[2], 1), 0, 1)
    sea_tile = draw_sea_tile(jax.random.fold_in(key_of[8], 71), 0)
    push_list = draw_push_list(jax.random.fold_in(key_of[8], 71), 0)
    neighbors = draw_neighbors(jax.random.fold_in(key_of[8], 71), 0)
    air_wind = normal_values(key_of[6], (2, NLAT, NLON), 1.0, 6.0, ((1, 8), (2, 16)), jnp.float32)
    diffusion = jnp.clip(jnp.exp(math.log(0.2) - 1.609438 * jax.random.uniform(key_of[7], (NLAT, NLON), jnp.float32) ** levels(key_of[7], (NLAT, NLON), ((0, 8), (1, 16)), -0.2, 0.2)), 0.04, 0.2)
    return dict(spectra=spectra, interact=interact, sea_mask=sea_mask, sea_tile=sea_tile, push_list=push_list, neighbors=neighbors, air_wind=air_wind, diffusion=diffusion)


def spectral_tables():
    component = jnp.arange(ND * NF, dtype=jnp.int32)
    freq_index = (component // ND).astype(jnp.float32)
    dir_index = (component % ND).astype(jnp.float32)
    angles = (dir_index + 0.5) * (2.0 * math.pi / ND)
    cosine = jnp.cos(angles)[:, None]
    sine = jnp.sin(angles)[:, None]
    scale = jnp.power(1.1, freq_index - NF / 2)[:, None]
    reach = (0.7 * jnp.power(1.1, -freq_index))[:, None]
    return (cosine, sine, scale, reach)

def air_step(padded, spread, turning):
    interior = padded[:, 1:-1, 1:-1]
    laplace = padded[:, 2:, 1:-1] + padded[:, :-2, 1:-1] + padded[:, 1:-1, 2:] + padded[:, 1:-1, :-2] - 4.0 * interior
    east_wind = interior[0] + spread * laplace[0] + turning * interior[1]
    north_wind = interior[1] + spread * laplace[1] - turning * interior[0]
    return jnp.stack([east_wind, north_wind])

def slot_ranks(tile_rows, count):
    tile_hot = (tile_rows[:, None] == jnp.arange(count, dtype=jnp.int32)[None, :]).astype(jnp.int32)
    return (lax.optimization_barrier(jnp.sum(jnp.cumsum(tile_hot, axis=0) * tile_hot, axis=1)) - 1).astype(jnp.int32)

def sources(spectra, point_wind, sea_weight, interact, cosine, sine, scale):
    east_wind = point_wind[0:1].astype(jnp.float32)
    north_wind = point_wind[1:2].astype(jnp.float32)
    projected = cosine * east_wind + sine * north_wind
    growth = 0.5 * jnp.maximum(0.8 * scale * projected - 1.0, 0.0)
    energy = spectra.astype(jnp.float32)
    mean_energy = lax.optimization_barrier(jnp.mean(energy, axis=0, keepdims=True))
    whitecap = 0.3 * scale * scale * mean_energy / (1.0 + mean_energy)
    nonlinear = jnp.dot(interact, spectra, preferred_element_type=jnp.float32)
    sourced = (sea_weight * (energy + 0.5 * ((growth - whitecap) * energy + nonlinear))).astype(jnp.bfloat16)
    return (sourced, growth)

def propagate(extended, links, sea_weight, cosine, sine, reach):
    courant_x = reach * cosine
    courant_y = reach * sine
    block_width = links.shape[1]
    half_rim = (extended.shape[1] - block_width) // 2
    center = extended[:, half_rim:half_rim + block_width].astype(jnp.float32)
    west_side = jnp.take(extended, links[0], axis=1).astype(jnp.float32)
    east_side = jnp.take(extended, links[1], axis=1).astype(jnp.float32)
    south_side = jnp.take(extended, links[2], axis=1).astype(jnp.float32)
    north_side = jnp.take(extended, links[3], axis=1).astype(jnp.float32)
    updated = (1.0 - jnp.abs(courant_x) - jnp.abs(courant_y)) * center
    updated = updated + jnp.maximum(courant_x, 0.0) * west_side + jnp.maximum(-courant_x, 0.0) * east_side
    updated = updated + jnp.maximum(courant_y, 0.0) * south_side + jnp.maximum(-courant_y, 0.0) * north_side
    return (sea_weight * updated).astype(jnp.bfloat16)

def stresses(spectra, growth, point_wind, sea_weight, cosine, sine, scale):
    lifting = growth * spectra.astype(jnp.float32) * scale
    wave_x = 0.2 * lax.optimization_barrier(jnp.mean(lifting * cosine, axis=0))
    wave_y = 0.2 * lax.optimization_barrier(jnp.mean(lifting * sine, axis=0))
    east_wind = point_wind[0].astype(jnp.float32)
    north_wind = point_wind[1].astype(jnp.float32)
    wind_speed = jnp.sqrt(east_wind * east_wind + north_wind * north_wind + 0.25)
    water = sea_weight[0]
    stress_x = water * (0.3 * wind_speed * east_wind + wave_x)
    stress_y = water * (0.3 * wind_speed * north_wind + wave_y)
    roughness_pts = water * 0.2 * jnp.sqrt(stress_x * stress_x + stress_y * stress_y + 0.01)
    return jnp.stack([stress_x, stress_y, roughness_pts, water])

def reference(spectra, interact, sea_mask, sea_tile, push_list, neighbors, air_wind, diffusion):
    cosine, sine, scale, reach = spectral_tables()
    turning = (0.05 + 0.1 * jnp.arange(NLAT, dtype=jnp.int32).astype(jnp.float32) / NLAT)[:, None]
    air_state = air_wind
    for substep in range(ATM_STEPS):
        air_state = air_step(jnp.pad(air_state, ((0, 0), (1, 1), (1, 1))), diffusion, turning)
    tile_rows = sea_tile.reshape(BLOCKS, P_DEV)
    ranked = lax.map(lambda tiles: slot_ranks(tiles, BLOCKS), tile_rows)
    block_ids = jnp.arange(BLOCKS, dtype=jnp.int32)[:, None]
    cell_index = push_list[tile_rows, block_ids, ranked]
    row_index = (tile_rows % N_ATM * LAT_DEV + cell_index // LON_DEV).reshape(-1)
    col_index = (tile_rows // N_ATM * LON_DEV + cell_index % LON_DEV).reshape(-1)
    point_wind = air_state[:, row_index, col_index].astype(jnp.bfloat16)
    sea_weight = sea_mask.astype(jnp.float32).reshape(BLOCKS, 1, P_DEV)
    block_spectra = spectra.reshape(K, BLOCKS, P_DEV).transpose(1, 0, 2)
    block_wind = point_wind.reshape(2, BLOCKS, P_DEV).transpose(1, 0, 2)

    def per_block(inputs):
        state, winds, weight = inputs
        sourced, growth = sources(state, winds, weight, interact, cosine, sine, scale)
        return (sourced, stresses(state, growth, winds, weight, cosine, sine, scale))
    sourced_blocks, coupled = lax.map(per_block, (block_spectra, block_wind, sea_weight))
    whole = sourced_blocks.transpose(1, 0, 2).reshape(K, NPTS)
    padded = jnp.pad(whole, ((0, 0), (H, H)))
    links = neighbors.reshape(4, BLOCKS, P_DEV).transpose(1, 0, 2)

    def moved(inputs):
        block, link_rows, weight = inputs
        extended = lax.dynamic_slice_in_dim(padded, block * P_DEV, P_DEV + 2 * H, 1)
        return propagate(extended, link_rows, weight, cosine, sine, reach)
    moved_blocks = lax.map(moved, (jnp.arange(BLOCKS, dtype=jnp.int32), links, sea_weight))
    wave_spectra = moved_blocks.transpose(1, 0, 2).reshape(K, NPTS)
    flat_cells = row_index * NLON + col_index
    coupled_all = coupled.transpose(1, 0, 2).reshape(4, NPTS)
    cell_sums = jnp.zeros((4, NLAT * NLON), jnp.float32).at[:, flat_cells].add(coupled_all)
    cell_count = jnp.maximum(cell_sums[3], 1.0)
    surface_wind = air_state - 0.5 * (cell_sums[:2] / cell_count).reshape(2, NLAT, NLON)
    roughness = (cell_sums[2] / cell_count).reshape(NLAT, NLON)
    return (wave_spectra, surface_wind, roughness)
```

```python
import math

import jax
import jax.numpy as jnp
import numpy as np
from jax import lax
from jax.experimental import pallas as pl
from jax.experimental.pallas import tpu as pltpu
from jax.sharding import PartitionSpec as P

ND = 36
NF = 36
K = ND * NF
H = 512
ATM_STEPS = 4
TW = 256
CH = 144
NCH = K // CH
HALF = 72
HALO_ROWS = K + 16
F32 = jnp.float32
BF16 = jnp.bfloat16
I32 = jnp.int32

S_TILES = (0, 1, 2, 4, 5, 6)
N_TILES = (2, 3, 4, 6, 7, 8)
PICK = 8 * len(S_TILES)


def row_tables():
    r = np.arange(HALF)
    d = r % ND
    angle = (d + 0.5) * (2.0 * math.pi / ND)
    up = np.power(1.1, r // ND)
    cosine, sine = np.cos(angle), np.sin(angle)
    reach = 0.7 / up
    rows = [
        up * cosine,
        up * sine,
        np.abs(reach * cosine),
        np.abs(reach * sine),
        np.abs(reach * cosine) + np.abs(reach * sine),
        (cosine > 0).astype(np.float64),
        (sine > 0).astype(np.float64),
    ]
    table = np.stack(rows).astype(np.float32)
    return np.ascontiguousarray(np.broadcast_to(table[:, :, None], table.shape + (128,)))


COS_POS = [bool(math.cos((d + 0.5) * 2.0 * math.pi / ND) > 0) for d in range(ND)]


def west_kind(tile):
    signs = {COS_POS[(8 * tile + s) % ND] for s in range(8)}
    return "both" if len(signs) == 2 else ("west" if True in signs else "east")


def iota(shape, dim):
    return lax.broadcasted_iota(I32, shape, dim)


def hot(mask):
    return jnp.where(mask, 1.0, 0.0).astype(BF16)


def contract(a, b, da, db):
    return lax.dot_general(a, b, (((da,), (db,)), ((), ())), preferred_element_type=F32)


def params(megabytes):
    return pltpu.CompilerParams(vmem_limit_bytes=megabytes << 20)


def cost(flops, data):
    return pl.CostEstimate(flops=flops, bytes_accessed=data, transcendentals=0)


def prepare_kernel(tile_ref, mask_ref, push_ref, first_ref, last_ref, pts_ref, pusht_ref, to_prev, to_next):
    blocks = push_ref.shape[0]
    points = tile_ref.shape[1]
    pusht_ref[...] = push_ref[...].astype(F32).T.astype(I32)
    before = hot(iota((TW, TW), 0) < iota((TW, TW), 1))
    ones = jnp.ones((TW, TW), BF16)
    running = jnp.zeros((blocks, TW), F32)
    for c in range(points // TW):
        cols = slice(c * TW, (c + 1) * TW)
        tile = tile_ref[:, cols]
        same = iota((blocks, TW), 0) == tile
        onehot = hot(same)
        earlier = contract(onehot, before, 1, 0) + running
        rank = jnp.sum(jnp.where(same, earlier, 0.0), axis=0, keepdims=True)
        running = running + contract(onehot, ones, 1, 0)
        pts_ref[0:1, cols] = tile.astype(F32)
        pts_ref[1:2, cols] = rank
        pts_ref[2:3, cols] = mask_ref[:, cols].astype(F32)
        pts_ref[3:8, cols] = jnp.zeros((5, TW), F32)
    for out, src, lo in ((to_prev, first_ref, 0), (to_next, last_ref, points - H)):
        out[:K, :] = src[...]
        rows = jnp.concatenate([pts_ref[:, lo : lo + H], jnp.zeros((8, H), F32)], axis=0)
        out[K:, :] = rows.astype(BF16)


def prepare(tile, mask, push, spectra):
    blocks, capacity = push.shape
    points = tile.shape[1]
    last = points // H - 1
    whole = lambda *shape: pl.BlockSpec(shape, lambda i: (0,) * len(shape))
    return pl.pallas_call(
        prepare_kernel,
        grid=(1,),
        in_specs=[
            whole(1, points),
            whole(1, points),
            whole(blocks, capacity),
            pl.BlockSpec((K, H), lambda i: (0, 0)),
            pl.BlockSpec((K, H), lambda i: (0, last)),
        ],
        out_specs=[whole(8, points), whole(capacity, blocks), whole(HALO_ROWS, H), whole(HALO_ROWS, H)],
        out_shape=[
            jax.ShapeDtypeStruct((8, points), F32),
            jax.ShapeDtypeStruct((capacity, blocks), I32),
            jax.ShapeDtypeStruct((HALO_ROWS, H), BF16),
            jax.ShapeDtypeStruct((HALO_ROWS, H), BF16),
        ],
        compiler_params=params(32),
        cost_estimate=cost(2 * 2 * blocks * TW * points, 4 * HALO_ROWS * H * 2),
        name="prepare",
    )(tile, mask, push, spectra, spectra)


def base_tile(interact, s_ref, mask, out_ref):
    out_ref[...] = jnp.dot(interact[...], s_ref[...], preferred_element_type=F32)
    for lane in range(TW // 128):
        lanes = slice(lane * 128, (lane + 1) * 128)
        acc = jnp.zeros((HALF, 128), F32)
        for m in range(NCH):
            s = s_ref[m * CH : (m + 1) * CH, lanes].astype(F32)
            acc = acc + (s[:HALF] + s[HALF:])
        mean = jnp.sum(acc, axis=0, keepdims=True) * (1.0 / K)
        msk = jnp.broadcast_to(mask[:, lanes], (8, 128))
        quota = jnp.broadcast_to(mean / (1.0 + mean), (8, 128)) * msk * 0.15
        half = 0.5 * msk
        low = iota((8, 128), 0) < 4
        for m in range(NCH):
            s = s_ref[m * CH : (m + 1) * CH, lanes].astype(F32)
            n = out_ref[m * CH : (m + 1) * CH, lanes]
            keeps = []
            for h in range(2):
                power = 1.21 ** (4 * m + 2 * h - NF / 2)
                a = msk - power * quota
                b = msk - (1.21 * power) * quota
                keeps += [a] * 4 + [jnp.where(low, a, b)] + [b] * 4
            out = [
                s[8 * i : 8 * i + 8] * keep + n[8 * i : 8 * i + 8] * half for i, keep in enumerate(keeps)
            ]
            out_ref[m * CH : (m + 1) * CH, lanes] = jnp.concatenate(out, axis=0)


def base_kernel(it_ref, s_ref, p_ref, out_ref):
    base_tile(it_ref, s_ref, p_ref[2:3, :], out_ref)


def base_own(interact, spectra, pts):
    points = spectra.shape[1]
    return pl.pallas_call(
        base_kernel,
        grid=(points // TW,),
        in_specs=[
            pl.BlockSpec((K, K), lambda i: (0, 0), pipeline_mode=pl.Buffered(1)),
            pl.BlockSpec((K, TW), lambda i: (0, i)),
            pl.BlockSpec((8, TW), lambda i: (0, i)),
        ],
        out_specs=pl.BlockSpec((K, TW), lambda i: (0, i)),
        out_shape=jax.ShapeDtypeStruct((K, points), F32),
        compiler_params=params(32),
        cost_estimate=cost(2 * K * K * points, K * K * 2 + K * points * 6),
        name="base_own",
    )(interact, spectra, pts)


def base_halo_kernel(it_ref, sb_ref, sa_ref, pb_ref, pa_ref, out_ref):
    i = pl.program_id(0)

    @pl.when(i < H // TW)
    def _():
        base_tile(it_ref, sb_ref, pb_ref[...].astype(F32)[2:3, :], out_ref)

    @pl.when(i >= H // TW)
    def _():
        base_tile(it_ref, sa_ref, pa_ref[...].astype(F32)[2:3, :], out_ref)


def base_halo(interact, before, after):
    n = H // TW
    early = lambda i: jnp.minimum(i, n - 1)
    late = lambda i: jnp.maximum(i - n, 0)
    return pl.pallas_call(
        base_halo_kernel,
        grid=(2 * n,),
        in_specs=[
            pl.BlockSpec((K, K), lambda i: (0, 0), pipeline_mode=pl.Buffered(1)),
            pl.BlockSpec((K, TW), lambda i: (0, early(i))),
            pl.BlockSpec((K, TW), lambda i: (0, late(i))),
            pl.BlockSpec((16, TW), lambda i: (K // 16, early(i))),
            pl.BlockSpec((16, TW), lambda i: (K // 16, late(i))),
        ],
        out_specs=pl.BlockSpec((K, TW), lambda i: (0, i)),
        out_shape=jax.ShapeDtypeStruct((K, 2 * H), F32),
        compiler_params=params(32),
        cost_estimate=cost(2 * K * K * 2 * H, K * K * 2 + K * 2 * H * 6),
        name="base_halo",
    )(interact, before, after, before, after)


def air_kernel(lat_total, mid_ref, left_ref, right_ref, pusht_ref, air_ref, out_ref, slots):
    rows = mid_ref.shape[1]
    lat_dev = rows - 16
    lane = iota((rows, 128), 1)

    def field(i):
        side = jnp.where(lane < 8, right_ref[i], jnp.where(lane >= 120, left_ref[i], 0.0))
        return jnp.concatenate([mid_ref[i], side], axis=1)

    east, north, spread = field(0), field(1), field(2)
    first = lax.axis_index("atm") * lat_dev - 8
    row = (iota((rows, 256), 0) + first).astype(F32)
    turning = 0.05 + 0.1 * row / lat_total

    def laplace(w):
        around = pltpu.roll(w, rows - 1, 0) + pltpu.roll(w, 1, 0) + pltpu.roll(w, 255, 1) + pltpu.roll(w, 1, 1)
        return around - 4.0 * w

    for _ in range(ATM_STEPS):
        e = east + spread * laplace(east) + turning * north
        n = north + spread * laplace(north) - turning * east
        east, north = e, n
    east = east[8 : 8 + lat_dev, :128]
    north = north[8 : 8 + lat_dev, :128]
    air_ref[0] = east
    air_ref[1] = north
    field_t = jnp.concatenate([east.T, north.T], axis=0).astype(BF16)
    capacity, blocks = pusht_ref.shape
    group = 4
    for g in range(capacity // group):
        cells = jnp.concatenate([pusht_ref[g * group + k : g * group + k + 1, :] for k in range(group)], axis=1)
        at_row = hot(iota((lat_dev, group * blocks), 0) == (cells >> 7))
        picked = jnp.dot(field_t, at_row, preferred_element_type=F32)
        at_col = iota((128, group * blocks), 0) == (cells & 127)
        for c in range(2):
            value = jnp.sum(jnp.where(at_col, picked[c * 128 : (c + 1) * 128], 0.0), axis=0, keepdims=True)
            for k in range(group):
                at = c * capacity + g * group + k
                slots[at : at + 1, :] = value[:, k * blocks : (k + 1) * blocks]
    own = slots[...]
    stacked = jnp.concatenate([pltpu.roll(own, 1, 1), own, pltpu.roll(own, blocks - 1, 1), jnp.zeros_like(own)], axis=0)
    out_ref[...] = stacked.T.reshape(out_ref.shape)


def air(lat_total, mid, left, right, pusht):
    capacity, blocks = pusht.shape
    lat_dev = mid.shape[1] - 16
    assert mid.shape[2] == 128 and blocks == 128
    return pl.pallas_call(
        lambda *refs: air_kernel(lat_total, *refs),
        out_shape=[
            jax.ShapeDtypeStruct((2, lat_dev, 128), F32),
            jax.ShapeDtypeStruct((blocks, 1, 8 * capacity), F32),
        ],
        scratch_shapes=[pltpu.VMEM((2 * capacity, blocks), F32)],
        compiler_params=params(24),
        cost_estimate=cost(2 * 256 * lat_dev * capacity * blocks, 600000),
        name="air",
    )(mid, left, right, pusht)


def winds_at(table, tile, rank):
    slots = table.shape[0] // 2
    tiles = table.shape[1]
    points = tile.shape[1]
    onehot = hot(iota((tiles, points), 0) == tile.astype(I32))
    values = jnp.dot(table, onehot, preferred_element_type=F32)
    at = iota((slots, points), 0) == rank.astype(I32)
    east = jnp.sum(jnp.where(at, values[:slots], 0.0), axis=0, keepdims=True)
    north = jnp.sum(jnp.where(at, values[slots:], 0.0), axis=0, keepdims=True)
    return east, north, onehot, at


def growth_pattern(tab_ref, east, north):
    return tab_ref[0] * (0.2 * east) + tab_ref[1] * (0.2 * north)


def step_scale(m, h):
    return 1.1 ** (4 * m + 2 * h - NF / 2)


def source_kernel(tab_ref, got_ref, s_ref, base_ref, p_ref, out_ref, send_ref, table, total):
    i = pl.program_id(0)

    @pl.when(i == 0)
    def _():
        got = got_ref[...].reshape(got_ref.shape[0], got_ref.shape[2])
        table[...] = got.T[64:128, :].astype(BF16)
        total[...] = jnp.zeros_like(total)

    mask = p_ref[2:3, :]
    east, north, onehot, at = winds_at(table[...], p_ref[0:1, :], p_ref[1:2, :])
    wave_x, wave_y = [], []
    for lane in range(TW // 128):
        lanes = slice(lane * 128, (lane + 1) * 128)
        pattern = growth_pattern(tab_ref, east[:, lanes] * mask[:, lanes], north[:, lanes] * mask[:, lanes])
        acc = jnp.zeros((HALF, 128), F32)
        for m in range(NCH):
            s = s_ref[m * CH : (m + 1) * CH, lanes].astype(F32)
            b = base_ref[m * CH : (m + 1) * CH, lanes]
            out = []
            for h in range(2):
                scale = step_scale(m, h)
                half = slice(h * HALF, (h + 1) * HALF)
                grown = jnp.maximum(pattern - 0.25 / scale, 0.0) * s[half]
                out.append(b[half] + scale * grown)
                acc = acc + (scale * scale) * grown
            out_ref[m * CH : (m + 1) * CH, lanes] = jnp.concatenate(out, axis=0).astype(BF16)
        wave_x.append(jnp.sum(acc * tab_ref[0], axis=0, keepdims=True))
        wave_y.append(jnp.sum(acc * tab_ref[1], axis=0, keepdims=True))
    wave_x = jnp.concatenate(wave_x, axis=1) * (0.4 / K)
    wave_y = jnp.concatenate(wave_y, axis=1) * (0.4 / K)
    speed = jnp.sqrt(east * east + north * north + 0.25)
    stress_x = mask * (0.3 * speed * east + wave_x)
    stress_y = mask * (0.3 * speed * north + wave_y)
    rough = mask * 0.2 * jnp.sqrt(stress_x * stress_x + stress_y * stress_y + 0.01)
    values = jnp.concatenate([jnp.where(at, v, 0.0) for v in (stress_x, stress_y, rough, mask)], axis=0)
    high = values.astype(BF16)
    rest = values - high.astype(F32)
    middle = rest.astype(BF16)
    low = (rest - middle.astype(F32)).astype(BF16)
    total[...] += contract(
        jnp.concatenate([onehot] * 3, axis=1), jnp.concatenate([high, middle, low], axis=1), 1, 1
    )

    @pl.when(i == pl.num_programs(0) - 1)
    def _():
        send_ref[...] = total[...].reshape(send_ref.shape)


def sources(tab, got, spectra, base, pts):
    points = spectra.shape[1]
    blocks = got.shape[0]
    capacity = got.shape[2] // 8
    return pl.pallas_call(
        source_kernel,
        grid=(points // TW,),
        in_specs=[
            pl.BlockSpec(tab.shape, lambda i: (0, 0, 0), pipeline_mode=pl.Buffered(1)),
            pl.BlockSpec(got.shape, lambda i: (0, 0, 0), pipeline_mode=pl.Buffered(1)),
            pl.BlockSpec((K, TW), lambda i: (0, i)),
            pl.BlockSpec((K, TW), lambda i: (0, i)),
            pl.BlockSpec((8, TW), lambda i: (0, i)),
        ],
        out_specs=[
            pl.BlockSpec((K, TW), lambda i: (0, i)),
            pl.BlockSpec((blocks, 1, 4 * capacity), lambda i: (0, 0, 0)),
        ],
        out_shape=[
            jax.ShapeDtypeStruct((K, points), BF16),
            jax.ShapeDtypeStruct((blocks, 1, 4 * capacity), F32),
        ],
        scratch_shapes=[
            pltpu.VMEM((2 * capacity, blocks), BF16),
            pltpu.VMEM((blocks, 4 * capacity), F32),
        ],
        compiler_params=params(32),
        cost_estimate=cost(10 * K * points, K * points * 8),
        name="sources",
    )(tab, got, spectra, base, pts)


def move_kernel(
    tab_ref, got_ref, own_ref, bh_ref, sb_ref, sa_ref, pb_ref, pa_ref, link_ref, p_ref,
    out_ref, table, natural, south_rows, north_rows, south_y, north_y,
):
    q = pl.program_id(0)
    halo = H // TW
    tiles = pl.num_programs(0)
    lag = 2 * halo
    mine = pl.ds(pl.multiple_of(q * TW, TW), TW)

    @pl.when(q == 0)
    def _():
        got = got_ref[...].reshape(got_ref.shape[0], got_ref.shape[2])
        table[...] = got.T.astype(BF16)

    def keep(m, x):
        natural[m * CH : (m + 1) * CH, mine] = x.astype(BF16)
        for ref, chosen in ((south_rows, S_TILES), (north_rows, N_TILES)):
            rows = [x[HALF * h + 8 * t : HALF * h + 8 * t + 8] for h in range(2) for t in chosen]
            ref[m * 2 * PICK : (m + 1) * 2 * PICK, mine] = jnp.concatenate(rows, axis=0).astype(BF16)

    def halo_tile(s_ref, pts, shift):
        slots = table.shape[0] // 4
        mask = pts[2:3, :]
        east, north, _, _ = winds_at(table[shift * slots : (shift + 1) * slots, :], pts[0:1, :], pts[1:2, :])
        east, north = east * mask, north * mask
        patterns = [
            growth_pattern(tab_ref, east[:, l * 128 : l * 128 + 128], north[:, l * 128 : l * 128 + 128])
            for l in range(TW // 128)
        ]
        pattern = jnp.concatenate(patterns, axis=1)
        for m in range(NCH):
            s = s_ref[m * CH : (m + 1) * CH, :].astype(F32)
            b = bh_ref[m * CH : (m + 1) * CH, :]
            out = []
            for h in range(2):
                scale = step_scale(m, h)
                half = slice(h * HALF, (h + 1) * HALF)
                out.append(b[half] + scale * (jnp.maximum(pattern - 0.25 / scale, 0.0) * s[half]))
            keep(m, jnp.concatenate(out, axis=0))

    @pl.when(q < halo)
    def _():
        halo_tile(sb_ref, pb_ref[...].astype(F32), 0)

    @pl.when(jnp.logical_and(q >= halo, q < tiles - halo))
    def _():
        for m in range(NCH):
            keep(m, own_ref[m * CH : (m + 1) * CH, :].astype(F32))

    @pl.when(q >= tiles - halo)
    def _():
        halo_tile(sa_ref, pa_ref[...].astype(F32), 2)

    @pl.when(q >= lag)
    def _():
        j = q - lag
        width = TW + H
        first = pl.multiple_of(j * TW, TW)
        second = pl.multiple_of(j * TW + H, TW)
        south_hot = hot(iota((width, TW), 0) == link_ref[2:3, :] - first)
        south_y[...] = jnp.dot(south_rows[:, pl.ds(first, width)], south_hot, preferred_element_type=F32)
        north_hot = hot(iota((width, TW), 0) == link_ref[3:4, :] - second)
        north_y[...] = jnp.dot(north_rows[:, pl.ds(second, width)], north_hot, preferred_element_type=F32)
        mask = p_ref[2:3, :]
        lane = iota((8, 128), 1)
        for l in range(TW // 128):
            lanes = slice(l * 128, (l + 1) * 128)
            msk = jnp.broadcast_to(mask[:, lanes], (8, 128))
            near = [pl.ds(pl.multiple_of(second + (l + o) * 128, 128), 128) for o in (-1, 0, 1)]
            for m in range(NCH):
                rows = slice(m * CH, (m + 1) * CH)
                left, here, right = (natural[rows, at].astype(F32) for at in near)
                ys = south_y[m * 2 * PICK : (m + 1) * 2 * PICK, lanes]
                yn = north_y[m * 2 * PICK : (m + 1) * 2 * PICK, lanes]
                out = []
                for h in range(2):
                    shrink = 1.1 ** (-(4 * m + 2 * h))
                    for t in range(9):
                        at = HALF * h + 8 * t
                        c = here[at : at + 8]
                        kind = west_kind(t)
                        if kind != "east":
                            west = jnp.where(
                                lane == 0, pltpu.roll(left[at : at + 8], 1, 1), pltpu.roll(c, 1, 1)
                            )
                            x = west
                        if kind != "west":
                            east = jnp.where(
                                lane == 127, pltpu.roll(right[at : at + 8], 127, 1), pltpu.roll(c, 127, 1)
                            )
                            x = east
                        tr = slice(8 * t, 8 * t + 8)
                        if kind == "both":
                            x = jnp.where(tab_ref[5, tr] > 0, west, east)
                        if t in S_TILES:
                            k = PICK * h + 8 * S_TILES.index(t)
                            y = ys[k : k + 8]
                        if t in N_TILES:
                            k = PICK * h + 8 * N_TILES.index(t)
                            y = jnp.where(tab_ref[6, tr] > 0, y, yn[k : k + 8]) if t in S_TILES else yn[k : k + 8]
                        flow = (tab_ref[2, tr] * x + tab_ref[3, tr] * y) * msk - tab_ref[4, tr] * c
                        out.append(c + shrink * flow)
                out_ref[rows, lanes] = jnp.concatenate(out, axis=0).astype(BF16)


def move(tab, got, own, base_h, before, after, links, pts):
    points = own.shape[1]
    halo = H // TW
    lag = 2 * halo
    mine = points // TW
    steps = mine + lag
    early = lambda q: jnp.minimum(q, halo - 1)
    late = lambda q: jnp.clip(q - mine - halo, 0, halo - 1)
    out_at = lambda q: jnp.clip(q - lag, 0, mine - 1)
    both = lambda q: jnp.where(q < mine + halo, early(q), halo + late(q))
    extended = points + 2 * H
    return pl.pallas_call(
        move_kernel,
        grid=(steps,),
        in_specs=[
            pl.BlockSpec(tab.shape, lambda q: (0, 0, 0), pipeline_mode=pl.Buffered(1)),
            pl.BlockSpec(got.shape, lambda q: (0, 0, 0), pipeline_mode=pl.Buffered(1)),
            pl.BlockSpec((K, TW), lambda q: (0, jnp.clip(q - halo, 0, mine - 1))),
            pl.BlockSpec((K, TW), lambda q: (0, both(q))),
            pl.BlockSpec((K, TW), lambda q: (0, early(q))),
            pl.BlockSpec((K, TW), lambda q: (0, late(q))),
            pl.BlockSpec((16, TW), lambda q: (K // 16, early(q))),
            pl.BlockSpec((16, TW), lambda q: (K // 16, late(q))),
            pl.BlockSpec((4, TW), lambda q: (0, out_at(q))),
            pl.BlockSpec((8, TW), lambda q: (0, out_at(q))),
        ],
        out_specs=pl.BlockSpec((K, TW), lambda q: (0, out_at(q))),
        out_shape=jax.ShapeDtypeStruct((K, points), BF16),
        scratch_shapes=[
            pltpu.VMEM((got.shape[2], got.shape[0]), BF16),
            pltpu.VMEM((K, extended), BF16),
            pltpu.VMEM((18 * PICK, extended), BF16),
            pltpu.VMEM((18 * PICK, extended), BF16),
            pltpu.VMEM((18 * PICK, TW), F32),
            pltpu.VMEM((18 * PICK, TW), F32),
        ],
        compiler_params=params(48),
        cost_estimate=cost(2 * 2 * 18 * PICK * (TW + H) * points, K * points * 8),
        name="move",
    )(tab, got, own, base_h, before, after, before, after, links, pts)


def cell_kernel(got_ref, push_ref, pusht_ref, air_ref, wind_ref, rough_ref, left, right):
    capacity, blocks = pusht_ref.shape
    lat_dev = air_ref.shape[1]
    values = got_ref[...].reshape(blocks, 4 * capacity).T
    high = values.astype(BF16).astype(F32)
    low = values - high
    for r in range(capacity):
        cols = slice(r * blocks, (r + 1) * blocks)
        at_row = iota((lat_dev, blocks), 0) == (pusht_ref[r : r + 1, :] >> 7)
        for part, source in enumerate((high, low)):
            rows = [
                jnp.where(at_row, source[c * capacity + r : c * capacity + r + 1, :], 0.0) for c in range(4)
            ]
            left[part * 4 * lat_dev : (part + 1) * 4 * lat_dev, cols] = jnp.concatenate(rows, axis=0).astype(BF16)
        right[cols, :] = hot(iota((blocks, 128), 1) == (push_ref[:, r : r + 1] & 127))
    sums = jnp.dot(left[...], right[...], preferred_element_type=F32)
    sums = sums[: 4 * lat_dev] + sums[4 * lat_dev :]
    sx, sy, rough, share = (sums[c * lat_dev : (c + 1) * lat_dev] for c in range(4))
    count = jnp.maximum(share, 1.0)
    wind_ref[0] = air_ref[0] - 0.5 * (sx / count)
    wind_ref[1] = air_ref[1] - 0.5 * (sy / count)
    rough_ref[...] = rough / count


def cells(got, push, pusht, air_state):
    capacity, blocks = pusht.shape
    lat_dev = air_state.shape[1]
    return pl.pallas_call(
        cell_kernel,
        out_shape=[
            jax.ShapeDtypeStruct(air_state.shape, F32),
            jax.ShapeDtypeStruct(air_state.shape[1:], F32),
        ],
        scratch_shapes=[
            pltpu.VMEM((8 * lat_dev, capacity * blocks), BF16),
            pltpu.VMEM((capacity * blocks, 128), BF16),
        ],
        compiler_params=params(24),
        cost_estimate=cost(2 * 8 * lat_dev * 128 * capacity * blocks, 400000),
        name="cells",
    )(got, push, pusht, air_state)


def chain(axis, step):
    peers = lax.axis_size(axis)
    pairs = [(i, i + 1) for i in range(peers - 1)]
    return pairs if step > 0 else [(j, i) for i, j in pairs]


def shards(spectra, interact, sea_mask, sea_tile, push_list, neighbors, air_wind, diffusion):
    both = ("wave", "atm")
    tab = jnp.asarray(row_tables())
    lat_total = air_wind.shape[1] * lax.axis_size("atm")
    points = spectra.shape[1]
    push = push_list[0]

    pack = jnp.concatenate([air_wind, diffusion[None]], axis=0)
    above = lax.ppermute(pack[:, -8:], "atm", chain("atm", 1))
    below = lax.ppermute(pack[:, :8], "atm", chain("atm", -1))
    mid = jnp.concatenate([above, pack, below], axis=1)
    left = lax.ppermute(mid, "wave", chain("wave", 1))
    right = lax.ppermute(mid, "wave", chain("wave", -1))

    pts, pusht, to_prev, to_next = prepare(
        sea_tile.reshape(1, points), sea_mask.reshape(1, points), push, spectra
    )
    before = lax.ppermute(to_next, both, chain(both, 1))
    after = lax.ppermute(to_prev, both, chain(both, -1))

    air_state, outgoing = air(lat_total, mid, left, right, pusht)
    arrived = lax.all_to_all(outgoing, both, split_axis=0, concat_axis=0, tiled=True)

    base = base_own(interact, spectra, pts)
    base_h = base_halo(interact, before, after)
    sourced, outbound = sources(tab, arrived, spectra, base, pts)
    inbound = lax.all_to_all(outbound, both, split_axis=0, concat_axis=0, tiled=True)
    wave_spectra = move(tab, arrived, sourced, base_h, before, after, neighbors, pts)
    surface_wind, roughness = cells(inbound, push, pusht, air_state)
    return (wave_spectra, surface_wind, roughness)


def solution(mesh):
    placed = (
        P(None, ("wave", "atm")),
        P(),
        P(("wave", "atm")),
        P(("wave", "atm")),
        P(("wave", "atm"), None, None),
        P(None, ("wave", "atm")),
        P(None, "atm", "wave"),
        P("atm", "wave"),
    )
    return jax.shard_map(
        shards,
        mesh=mesh,
        in_specs=placed,
        out_specs=(P(None, ("wave", "atm")), P(None, "atm", "wave"), P("atm", "wave")),
        check_vma=False,
    )
```

```python
import math

import jax
import jax.numpy as jnp
import numpy as np
from jax import lax
from jax.experimental import pallas as pl
from jax.experimental.pallas import tpu as pltpu
from jax.sharding import PartitionSpec as P

ND = 36
NF = 36
K = ND * NF
H = 512
ATM_STEPS = 4
TW = 256
CH = 144
NCH = K // CH
HALF = 72
HALO_ROWS = K + 16
F32 = jnp.float32
BF16 = jnp.bfloat16
I32 = jnp.int32

S_TILES = (0, 1, 2, 4, 5, 6)
N_TILES = (2, 3, 4, 6, 7, 8)
PICK = 8 * len(S_TILES)


def row_tables():
    r = np.arange(HALF)
    d = r % ND
    angle = (d + 0.5) * (2.0 * math.pi / ND)
    up = np.power(1.1, r // ND)
    cosine, sine = np.cos(angle), np.sin(angle)
    reach = 0.7 / up
    rows = [
        up * cosine,
        up * sine,
        np.abs(reach * cosine),
        np.abs(reach * sine),
        np.abs(reach * cosine) + np.abs(reach * sine),
        (cosine > 0).astype(np.float64),
        (sine > 0).astype(np.float64),
    ]
    table = np.stack(rows).astype(np.float32)
    return np.ascontiguousarray(np.broadcast_to(table[:, :, None], table.shape + (128,)))


COS_POS = [bool(math.cos((d + 0.5) * 2.0 * math.pi / ND) > 0) for d in range(ND)]


def west_kind(tile):
    signs = {COS_POS[(8 * tile + s) % ND] for s in range(8)}
    return "both" if len(signs) == 2 else ("west" if True in signs else "east")


def iota(shape, dim):
    return lax.broadcasted_iota(I32, shape, dim)


def hot(mask):
    return jnp.where(mask, 1.0, 0.0).astype(BF16)


def contract(a, b, da, db):
    return lax.dot_general(a, b, (((da,), (db,)), ((), ())), preferred_element_type=F32)


def params(megabytes):
    return pltpu.CompilerParams(vmem_limit_bytes=megabytes << 20)


BIG = 52


HERE = pl.BlockSpec(memory_space=pltpu.VMEM)
AWAY = pl.BlockSpec(memory_space=pl.ANY)


def cost(flops, data):
    return pl.CostEstimate(flops=flops, bytes_accessed=data, transcendentals=0)


def prepare_kernel(tile_ref, mask_ref, push_ref, s_ref, pts_ref, pusht_ref, to_prev, to_next, rims, sems):
    blocks = push_ref.shape[0]
    points = tile_ref.shape[1]
    ends = ((to_prev, 0), (to_next, points - H))
    loads = [
        pltpu.make_async_copy(s_ref.at[:, pl.ds(lo, H)], rims.at[k, pl.ds(0, K), :], sems.at[k])
        for k, (out, lo) in enumerate(ends)
    ]
    for load in loads:
        load.start()
    pusht_ref[...] = push_ref[...].astype(F32).T.astype(I32)
    before = hot(iota((TW, TW), 0) < iota((TW, TW), 1))
    ones = jnp.ones((TW, TW), BF16)
    running = jnp.zeros((blocks, TW), F32)
    for c in range(points // TW):
        cols = slice(c * TW, (c + 1) * TW)
        tile = tile_ref[:, cols]
        same = iota((blocks, TW), 0) == tile
        onehot = hot(same)
        earlier = contract(onehot, before, 1, 0) + running
        rank = jnp.sum(jnp.where(same, earlier, 0.0), axis=0, keepdims=True)
        running = running + contract(onehot, ones, 1, 0)
        pts_ref[0:1, cols] = tile.astype(F32)
        pts_ref[1:2, cols] = rank
        pts_ref[2:3, cols] = mask_ref[:, cols].astype(F32)
        pts_ref[3:8, cols] = jnp.zeros((5, TW), F32)
    stores = []
    for k, (out, lo) in enumerate(ends):
        rows = jnp.concatenate([pts_ref[:, lo : lo + H], jnp.zeros((8, H), F32)], axis=0)
        rims[k, K:, :] = rows.astype(BF16)
        loads[k].wait()
        store = pltpu.make_async_copy(rims.at[k], out, sems.at[2 + k])
        store.start()
        stores.append(store)
    for store in stores:
        store.wait()


def prepare(tile, mask, push, spectra):
    blocks, capacity = push.shape
    points = tile.shape[1]
    return pl.pallas_call(
        prepare_kernel,
        in_specs=[HERE, HERE, HERE, AWAY],
        out_specs=[HERE, HERE, AWAY, AWAY],
        out_shape=[
            jax.ShapeDtypeStruct((8, points), F32),
            jax.ShapeDtypeStruct((capacity, blocks), I32),
            jax.ShapeDtypeStruct((HALO_ROWS, H), BF16),
            jax.ShapeDtypeStruct((HALO_ROWS, H), BF16),
        ],
        scratch_shapes=[pltpu.VMEM((2, HALO_ROWS, H), BF16), pltpu.SemaphoreType.DMA((4,))],
        compiler_params=params(BIG),
        cost_estimate=cost(2 * 2 * blocks * TW * points, 4 * HALO_ROWS * H * 2),
        name="prepare",
    )(tile, mask, push, spectra)


def base_tile(it_ref, s_ref, mask, out_ref, parts):
    depth = K // 3

    def multiply(c):
        rows = slice(c * depth, (c + 1) * depth)
        parts[rows, :] = jnp.dot(it_ref[rows, :], s_ref[...], preferred_element_type=F32)

    multiply(0)
    acc = jnp.zeros((HALF, TW), F32)
    for m in range(NCH):
        s = s_ref[m * CH : (m + 1) * CH, :].astype(F32)
        acc = acc + (s[:HALF] + s[HALF:])
    mean = jnp.sum(acc, axis=0, keepdims=True) * (1.0 / K)
    msk = jnp.broadcast_to(mask, (8, TW))
    quota = jnp.broadcast_to(mean / (1.0 + mean), (8, TW)) * msk * 0.15
    half = 0.5 * msk
    low = iota((8, TW), 0) < 4
    for c in range(3):
        if c < 2:
            multiply(c + 1)
        for m in range(3 * c, 3 * c + 3):
            rows = slice(m * CH, (m + 1) * CH)
            s = s_ref[rows, :].astype(F32)
            n = parts[rows, :]
            keeps = []
            for h in range(2):
                power = 1.21 ** (4 * m + 2 * h - NF / 2)
                a = msk - power * quota
                b = msk - (1.21 * power) * quota
                keeps += [a] * 4 + [jnp.where(low, a, b)] + [b] * 4
            out = [
                s[8 * i : 8 * i + 8] * keep + n[8 * i : 8 * i + 8] * half for i, keep in enumerate(keeps)
            ]
            out_ref[rows, :] = jnp.concatenate(out, axis=0)


def base_kernel(it_ref, s_ref, mask_ref, wait_ref, out_ref, parts):
    base_tile(it_ref, s_ref, mask_ref[...].astype(F32), out_ref, parts)


def base_own(interact, spectra, mask, first, count, wait):
    return pl.pallas_call(
        base_kernel,
        grid=(count,),
        in_specs=[
            pl.BlockSpec((K, K), lambda i: (0, 0), pipeline_mode=pl.Buffered(1)),
            pl.BlockSpec((K, TW), lambda i: (0, i + first)),
            pl.BlockSpec((1, TW), lambda i: (0, i + first)),
            AWAY,
        ],
        out_specs=pl.BlockSpec((K, TW), lambda i: (0, i)),
        out_shape=jax.ShapeDtypeStruct((K, count * TW), F32),
        scratch_shapes=[pltpu.VMEM((K, TW), F32)],
        compiler_params=params(BIG),
        cost_estimate=cost(2 * K * K * count * TW, K * K * 2),
        name="base_own",
    )(interact, spectra, mask, wait)


def base_halo_kernel(it_ref, sb_ref, sa_ref, pb_ref, pa_ref, wait_ref, out_ref, parts):
    i = pl.program_id(0)

    @pl.when(i < H // TW)
    def _():
        base_tile(it_ref, sb_ref, pb_ref[...].astype(F32)[2:3, :], out_ref, parts)

    @pl.when(i >= H // TW)
    def _():
        base_tile(it_ref, sa_ref, pa_ref[...].astype(F32)[2:3, :], out_ref, parts)


def base_halo(interact, before, after, wait):
    n = H // TW
    early = lambda i: jnp.minimum(i, n - 1)
    late = lambda i: jnp.maximum(i - n, 0)
    return pl.pallas_call(
        base_halo_kernel,
        grid=(2 * n,),
        in_specs=[
            pl.BlockSpec((K, K), lambda i: (0, 0), pipeline_mode=pl.Buffered(1)),
            pl.BlockSpec((K, TW), lambda i: (0, early(i))),
            pl.BlockSpec((K, TW), lambda i: (0, late(i))),
            pl.BlockSpec((16, TW), lambda i: (K // 16, early(i))),
            pl.BlockSpec((16, TW), lambda i: (K // 16, late(i))),
            AWAY,
        ],
        out_specs=pl.BlockSpec((K, TW), lambda i: (0, i)),
        out_shape=jax.ShapeDtypeStruct((K, 2 * H), F32),
        scratch_shapes=[pltpu.VMEM((K, TW), F32)],
        compiler_params=params(BIG),
        cost_estimate=cost(2 * K * K * 2 * H, K * K * 2),
        name="base_halo",
    )(interact, before, after, before, after, wait)


def air_kernel(lat_total, mid_ref, left_ref, right_ref, pusht_ref, air_ref, out_ref, slots):
    rows = mid_ref.shape[1]
    lat_dev = rows - 16
    lane = iota((rows, 128), 1)

    def field(i):
        side = jnp.where(lane < 8, right_ref[i], jnp.where(lane >= 120, left_ref[i], 0.0))
        return jnp.concatenate([mid_ref[i], side], axis=1)

    east, north, spread = field(0), field(1), field(2)
    first = lax.axis_index("atm") * lat_dev - 8
    row = (iota((rows, 256), 0) + first).astype(F32)
    turning = 0.05 + 0.1 * row / lat_total

    def laplace(w):
        around = pltpu.roll(w, rows - 1, 0) + pltpu.roll(w, 1, 0) + pltpu.roll(w, 255, 1) + pltpu.roll(w, 1, 1)
        return around - 4.0 * w

    for _ in range(ATM_STEPS):
        e = east + spread * laplace(east) + turning * north
        n = north + spread * laplace(north) - turning * east
        east, north = e, n
    east = east[8 : 8 + lat_dev, :128]
    north = north[8 : 8 + lat_dev, :128]
    air_ref[0] = east
    air_ref[1] = north
    field_t = jnp.concatenate([east.T, north.T], axis=0).astype(BF16)
    capacity, blocks = pusht_ref.shape
    group = 4
    for g in range(capacity // group):
        cells = jnp.concatenate([pusht_ref[g * group + k : g * group + k + 1, :] for k in range(group)], axis=1)
        at_row = hot(iota((lat_dev, group * blocks), 0) == (cells >> 7))
        picked = jnp.dot(field_t, at_row, preferred_element_type=F32)
        at_col = iota((128, group * blocks), 0) == (cells & 127)
        for c in range(2):
            value = jnp.sum(jnp.where(at_col, picked[c * 128 : (c + 1) * 128], 0.0), axis=0, keepdims=True)
            for k in range(group):
                at = c * capacity + g * group + k
                slots[at : at + 1, :] = value[:, k * blocks : (k + 1) * blocks]
    own = slots[...]
    stacked = jnp.concatenate([pltpu.roll(own, 1, 1), own, pltpu.roll(own, blocks - 1, 1), jnp.zeros_like(own)], axis=0)
    out_ref[...] = stacked.T.reshape(out_ref.shape)


def air(lat_total, mid, left, right, pusht, wait):
    capacity, blocks = pusht.shape
    lat_dev = mid.shape[1] - 16
    assert mid.shape[2] == 128 and blocks == 128
    return pl.pallas_call(
        lambda a, b, c, d, wait, *refs: air_kernel(lat_total, a, b, c, d, *refs),
        in_specs=[HERE] * 4 + [AWAY],
        out_specs=[HERE] * 2,
        out_shape=[
            jax.ShapeDtypeStruct((2, lat_dev, 128), F32),
            jax.ShapeDtypeStruct((blocks, 1, 8 * capacity), F32),
        ],
        scratch_shapes=[pltpu.VMEM((2 * capacity, blocks), F32)],
        compiler_params=params(BIG),
        cost_estimate=cost(2 * 256 * lat_dev * capacity * blocks, 600000),
        name="air",
    )(mid, left, right, pusht, wait)


def winds_at(table, tile, rank):
    slots = table.shape[0] // 2
    tiles = table.shape[1]
    points = tile.shape[1]
    onehot = hot(iota((tiles, points), 0) == tile.astype(I32))
    values = jnp.dot(table, onehot, preferred_element_type=F32)
    at = iota((slots, points), 0) == rank.astype(I32)
    east = jnp.sum(jnp.where(at, values[:slots], 0.0), axis=0, keepdims=True)
    north = jnp.sum(jnp.where(at, values[slots:], 0.0), axis=0, keepdims=True)
    return east, north, onehot, at


def growth_pattern(tab_ref, east, north):
    return tab_ref[0] * (0.2 * east) + tab_ref[1] * (0.2 * north)


def step_scale(m, h):
    return 1.1 ** (4 * m + 2 * h - NF / 2)


SW = 512


def lane_tile(i):
    return pl.ds(pl.multiple_of(i * 128, 128), 128)


def stress_kernel(
    tab_ref, got_ref, p_ref, s_hbm, sb_hbm, sa_hbm, wait_ref, send_ref, winds_ref, s_ref, rim, table, waves, sems
):
    points = p_ref.shape[1]
    blocks = got_ref.shape[0]
    slots = got_ref.shape[2] // 4
    groups = points // SW
    rims = [
        pltpu.make_async_copy(ref.at[pl.ds(K, 16), :], rim.at[k], sems.at[groups + k])
        for k, ref in enumerate((sb_hbm, sa_hbm))
    ]
    loads = [
        pltpu.make_async_copy(s_hbm.at[:, pl.ds(g * SW, SW)], s_ref.at[:, pl.ds(g * SW, SW)], sems.at[g])
        for g in range(groups)
    ]
    for load in rims + loads:
        load.start()
    table[...] = got_ref[...].reshape(blocks, got_ref.shape[2]).T.astype(BF16)
    winds_ref[3:8, :] = jnp.zeros((5, winds_ref.shape[1]), F32)

    def place(shift, pts, first):
        cols = slice(first, first + SW)
        east, north, _, _ = winds_at(table[shift * slots : (shift + 1) * slots, :], pts[0:1], pts[1:2])
        mask = pts[2:3]
        winds_ref[0:1, cols] = east * mask
        winds_ref[1:2, cols] = north * mask
        winds_ref[2:3, cols] = mask

    for load in rims:
        load.wait()
    place(0, rim[0].astype(F32), 0)
    place(2, rim[1].astype(F32), H + points)
    for g in range(groups):
        place(1, p_ref[:, g * SW : (g + 1) * SW], H + g * SW)

    def tile(i, carry):
        at = lane_tile(i + H // 128)
        pattern = growth_pattern(tab_ref, winds_ref[0:1, at], winds_ref[1:2, at])
        acc = jnp.zeros((HALF, 128), F32)
        for m in range(NCH):
            s = s_ref[m * CH : (m + 1) * CH, lane_tile(i)].astype(F32)
            for h in range(2):
                scale = step_scale(m, h)
                bent = jnp.maximum((scale * scale) * pattern - 0.25 * scale, 0.0)
                acc = acc + bent * s[h * HALF : (h + 1) * HALF]
        waves[0:1, lane_tile(i)] = jnp.sum(acc * tab_ref[0], axis=0, keepdims=True)
        waves[1:2, lane_tile(i)] = jnp.sum(acc * tab_ref[1], axis=0, keepdims=True)
        return carry

    per = SW // 128
    for g in range(groups):
        loads[g].wait()
        lax.fori_loop(g * per, (g + 1) * per, tile, 0)

    total = jnp.zeros((blocks, 2 * slots), F32)
    for g in range(groups):
        cols = slice(g * SW, (g + 1) * SW)
        east, north, mask = (winds_ref[k : k + 1, H + g * SW : H + (g + 1) * SW] for k in range(3))
        speed = jnp.sqrt(east * east + north * north + 0.25)
        stress_x = 0.3 * speed * east + mask * (waves[0:1, cols] * (0.4 / K))
        stress_y = 0.3 * speed * north + mask * (waves[1:2, cols] * (0.4 / K))
        rough = mask * 0.2 * jnp.sqrt(stress_x * stress_x + stress_y * stress_y + 0.01)
        onehot = hot(iota((blocks, SW), 0) == p_ref[0:1, cols].astype(I32))
        at = iota((slots // 2, SW), 0) == p_ref[1:2, cols].astype(I32)
        values = jnp.concatenate([jnp.where(at, v, 0.0) for v in (stress_x, stress_y, rough, mask)], axis=0)
        high = values.astype(BF16)
        rest = values - high.astype(F32)
        middle = rest.astype(BF16)
        low = (rest - middle.astype(F32)).astype(BF16)
        total = total + contract(
            jnp.concatenate([onehot] * 3, axis=1), jnp.concatenate([high, middle, low], axis=1), 1, 1
        )
    send_ref[...] = total.reshape(send_ref.shape)


def stresses(tab, got, pts, spectra, before, after, wait):
    points = spectra.shape[1]
    blocks = got.shape[0]
    capacity = got.shape[2] // 8
    return pl.pallas_call(
        stress_kernel,
        in_specs=[HERE] * 3 + [AWAY] * 4,
        out_specs=[HERE] * 2,
        out_shape=[
            jax.ShapeDtypeStruct((blocks, 1, 4 * capacity), F32),
            jax.ShapeDtypeStruct((8, points + 2 * H), F32),
        ],
        scratch_shapes=[
            pltpu.VMEM((K, points), BF16),
            pltpu.VMEM((2, 16, H), BF16),
            pltpu.VMEM((8 * capacity, blocks), BF16),
            pltpu.VMEM((8, points), F32),
            pltpu.SemaphoreType.DMA((points // SW + 2,)),
        ],
        compiler_params=params(BIG),
        cost_estimate=cost(10 * K * points, K * points * 2),
        name="stress",
    )(tab, got, pts, spectra, before, after, wait)


def chosen_rows(x, tiles):
    rows = [x[HALF * h + 8 * t : HALF * h + 8 * t + 8] for h in range(2) for t in tiles]
    return jnp.concatenate(rows, axis=0).astype(BF16)


def move_kernel(
    tab_ref, winds_ref, link_ref, s_hbm, sb_hbm, sa_hbm, b_hbm, bh_hbm,
    out_hbm, token, s_ref, b_ref, natural, south, north, staged, south_y, north_y, flows, sems,
):
    points = link_ref.shape[1]
    parts = points // H + 2
    loads = []
    for g in range(parts):
        to = pl.ds(g * H, H)
        if g == 0:
            pair = (sb_hbm.at[pl.ds(0, K), :], bh_hbm.at[:, pl.ds(0, H)])
        elif g == parts - 1:
            pair = (sa_hbm.at[pl.ds(0, K), :], bh_hbm.at[:, pl.ds(H, H)])
        else:
            own = pl.ds((g - 1) * H, H)
            pair = (s_hbm.at[:, own], b_hbm.at[:, own])
        loads.append(pltpu.make_async_copy(pair[0], s_ref.at[:, to], sems.at[2 * g]))
        loads.append(pltpu.make_async_copy(pair[1], b_ref.at[:, to], sems.at[2 * g + 1]))
    for load in loads:
        load.start()
    token[...] = jnp.zeros_like(token)

    def fill(i, kinds):
        at = lane_tile(i)
        pattern = growth_pattern(tab_ref, winds_ref[0:1, at], winds_ref[1:2, at])
        for m in range(NCH):
            rows = slice(m * CH, (m + 1) * CH)
            s = s_ref[rows, at].astype(F32)
            b = b_ref[rows, at]
            out = []
            for h in range(2):
                scale = step_scale(m, h)
                half = slice(h * HALF, (h + 1) * HALF)
                out.append(b[half] + jnp.maximum(scale * pattern - 0.25, 0.0) * s[half])
            x = jnp.concatenate(out, axis=0)
            natural[rows, at] = x.astype(BF16)
            picks = slice(m * 2 * PICK, (m + 1) * 2 * PICK)
            if "s" in kinds:
                south[picks, at] = chosen_rows(x, S_TILES)
            if "n" in kinds:
                north[picks, lane_tile(i - H // 128)] = chosen_rows(x, N_TILES)

    per = H // 128

    def fill_part(g, kinds):
        def body(i, carry):
            fill(i, kinds)
            return carry

        lax.fori_loop(g * per, (g + 1) * per, body, 0)

    def wait_part(g):
        loads[2 * g].wait()
        loads[2 * g + 1].wait()

    def output(j):
        width = TW + H
        window = pl.ds(pl.multiple_of(j * TW, TW), width)
        mine = pl.ds(pl.multiple_of(j * TW, TW), TW)
        south_hot = hot(iota((width, TW), 0) == link_ref[2:3, mine] - j * TW)
        north_hot = hot(iota((width, TW), 0) == link_ref[3:4, mine] - (j * TW + H))
        south_y[...] = jnp.dot(south[:, window], south_hot, preferred_element_type=F32)
        north_y[...] = jnp.dot(north[:, window], north_hot, preferred_element_type=F32)
        first = j * (TW // 128) + per
        for l in range(TW // 128):
            msk = winds_ref[2:3, lane_tile(first + l)]
            flows[l, 0] = tab_ref[2] * msk
            flows[l, 1] = tab_ref[3] * msk
        lane = iota((8, 128), 1)
        for l in range(TW // 128):
            lanes = slice(l * 128, (l + 1) * 128)
            for m in range(NCH):
                rows = slice(m * CH, (m + 1) * CH)
                left, here, right = (natural[rows, lane_tile(first + l + o)].astype(F32) for o in (-1, 0, 1))
                ys = south_y[m * 2 * PICK : (m + 1) * 2 * PICK, lanes]
                yn = north_y[m * 2 * PICK : (m + 1) * 2 * PICK, lanes]
                out = []
                for h in range(2):
                    shrink = 1.1 ** (-(4 * m + 2 * h))
                    for t in range(9):
                        at = HALF * h + 8 * t
                        c = here[at : at + 8]
                        kind = west_kind(t)
                        if kind != "east":
                            west = jnp.where(lane == 0, pltpu.roll(left[at : at + 8], 1, 1), pltpu.roll(c, 1, 1))
                            x = west
                        if kind != "west":
                            east = jnp.where(lane == 127, pltpu.roll(right[at : at + 8], 127, 1), pltpu.roll(c, 127, 1))
                            x = east
                        tr = slice(8 * t, 8 * t + 8)
                        if kind == "both":
                            x = jnp.where(tab_ref[5, tr] > 0, west, east)
                        if t in S_TILES:
                            k = PICK * h + 8 * S_TILES.index(t)
                            y = ys[k : k + 8]
                        if t in N_TILES:
                            k = PICK * h + 8 * N_TILES.index(t)
                            y = jnp.where(tab_ref[6, tr] > 0, y, yn[k : k + 8]) if t in S_TILES else yn[k : k + 8]
                        flow = flows[l, 0, tr] * x + flows[l, 1, tr] * y - tab_ref[4, tr] * c
                        out.append(c + shrink * flow)
                staged[rows, lane_tile(j * (TW // 128) + l)] = jnp.concatenate(out, axis=0).astype(BF16)

    def stores(j):
        at = pl.ds(j * TW, TW)
        return pltpu.make_async_copy(staged.at[:, at], out_hbm.at[:, at], sems.at[2 * parts + j])

    pair = H // TW
    wait_part(0)
    fill_part(0, "s")
    wait_part(1)
    fill_part(1, "sn")
    for g in range(2, parts):
        wait_part(g)
        fill_part(g, "n" if g == parts - 1 else "sn")
        lax.fori_loop((g - 2) * pair, (g - 1) * pair, lambda j, c: (output(j), c)[1], 0)
        for j in range((g - 2) * pair, (g - 1) * pair):
            stores(j).start()
    for j in range(points // TW):
        stores(j).wait()


def move(tab, winds, links, spectra, before, after, base, base_h):
    points = links.shape[1]
    extended = points + 2 * H
    return pl.pallas_call(
        move_kernel,
        in_specs=[HERE] * 3 + [AWAY] * 5,
        out_specs=[AWAY, HERE],
        out_shape=[jax.ShapeDtypeStruct((K, points), BF16), jax.ShapeDtypeStruct((8, 128), F32)],
        scratch_shapes=[
            pltpu.VMEM((K, extended), BF16),
            pltpu.VMEM((K, extended), F32),
            pltpu.VMEM((K, extended), BF16),
            pltpu.VMEM((18 * PICK, points + H), BF16),
            pltpu.VMEM((18 * PICK, points + H), BF16),
            pltpu.VMEM((K, points), BF16),
            pltpu.VMEM((18 * PICK, TW), F32),
            pltpu.VMEM((18 * PICK, TW), F32),
            pltpu.VMEM((TW // 128, 2, HALF, 128), F32),
            pltpu.SemaphoreType.DMA((2 * (points // H + 2) + points // TW,)),
        ],
        compiler_params=params(BIG),
        cost_estimate=cost(2 * 2 * 18 * PICK * (TW + H) * points, K * points * 8),
        name="move",
    )(tab, winds, links, spectra, before, after, base, base_h)


def cell_kernel(got_ref, push_ref, pusht_ref, air_ref, wait_ref, wind_ref, rough_ref, left, right):
    capacity, blocks = pusht_ref.shape
    lat_dev = air_ref.shape[1]
    values = got_ref[...].reshape(blocks, 4 * capacity).T
    high = values.astype(BF16).astype(F32)
    low = values - high
    for r in range(capacity):
        cols = slice(r * blocks, (r + 1) * blocks)
        at_row = iota((lat_dev, blocks), 0) == (pusht_ref[r : r + 1, :] >> 7)
        for part, source in enumerate((high, low)):
            rows = [
                jnp.where(at_row, source[c * capacity + r : c * capacity + r + 1, :], 0.0) for c in range(4)
            ]
            left[part * 4 * lat_dev : (part + 1) * 4 * lat_dev, cols] = jnp.concatenate(rows, axis=0).astype(BF16)
        right[cols, :] = hot(iota((blocks, 128), 1) == (push_ref[:, r : r + 1] & 127))
    sums = jnp.dot(left[...], right[...], preferred_element_type=F32)
    sums = sums[: 4 * lat_dev] + sums[4 * lat_dev :]
    sx, sy, rough, share = (sums[c * lat_dev : (c + 1) * lat_dev] for c in range(4))
    count = jnp.maximum(share, 1.0)
    wind_ref[0] = air_ref[0] - 0.5 * (sx / count)
    wind_ref[1] = air_ref[1] - 0.5 * (sy / count)
    rough_ref[...] = rough / count


def cells(got, push, pusht, air_state, wait):
    capacity, blocks = pusht.shape
    lat_dev = air_state.shape[1]
    return pl.pallas_call(
        cell_kernel,
        in_specs=[HERE] * 4 + [AWAY],
        out_specs=[HERE] * 2,
        out_shape=[
            jax.ShapeDtypeStruct(air_state.shape, F32),
            jax.ShapeDtypeStruct(air_state.shape[1:], F32),
        ],
        scratch_shapes=[
            pltpu.VMEM((8 * lat_dev, capacity * blocks), BF16),
            pltpu.VMEM((capacity * blocks, 128), BF16),
        ],
        compiler_params=params(BIG),
        cost_estimate=cost(2 * 8 * lat_dev * 128 * capacity * blocks, 400000),
        name="cells",
    )(got, push, pusht, air_state, wait)


def chain(axis, step):
    peers = lax.axis_size(axis)
    pairs = [(i, i + 1) for i in range(peers - 1)]
    return pairs if step > 0 else [(j, i) for i, j in pairs]


def shards(spectra, interact, sea_mask, sea_tile, push_list, neighbors, air_wind, diffusion):
    both = ("wave", "atm")
    tab = jnp.asarray(row_tables())
    lat_total = air_wind.shape[1] * lax.axis_size("atm")
    points = spectra.shape[1]
    tiles = points // TW
    push = push_list[0]
    mask = sea_mask.reshape(1, points)

    pack = jnp.concatenate([air_wind, diffusion[None]], axis=0)
    above = lax.ppermute(pack[:, -8:], "atm", chain("atm", 1))
    below = lax.ppermute(pack[:, :8], "atm", chain("atm", -1))
    mid = jnp.concatenate([above, pack, below], axis=1)
    left = lax.ppermute(mid, "wave", chain("wave", 1))
    right = lax.ppermute(mid, "wave", chain("wave", -1))

    pts, pusht, to_prev, to_next = prepare(sea_tile.reshape(1, points), mask, push, spectra)
    held, to_prev, to_next = lax.optimization_barrier((mid, to_prev, to_next))
    base = base_own(interact, spectra, mask, 0, tiles, held)
    before = lax.ppermute(to_next, both, chain(both, 1))
    after = lax.ppermute(to_prev, both, chain(both, -1))

    air_state, outgoing = air(lat_total, held, left, right, pusht, base)
    arrived = lax.all_to_all(outgoing, both, split_axis=0, concat_axis=0, tiled=True)
    base_h = base_halo(interact, before, after, outgoing)

    outbound, winds = stresses(tab, arrived, pts, spectra, before, after, base_h)
    inbound = lax.all_to_all(outbound, both, split_axis=0, concat_axis=0, tiled=True)
    wave_spectra, token = move(tab, winds, neighbors, spectra, before, after, base, base_h)
    surface_wind, roughness = cells(inbound, push, pusht, air_state, token)
    return (wave_spectra, surface_wind, roughness)


def solution(mesh):
    placed = (
        P(None, ("wave", "atm")),
        P(),
        P(("wave", "atm")),
        P(("wave", "atm")),
        P(("wave", "atm"), None, None),
        P(None, ("wave", "atm")),
        P(None, "atm", "wave"),
        P("atm", "wave"),
    )
    return jax.shard_map(
        shards,
        mesh=mesh,
        in_specs=placed,
        out_specs=(P(None, ("wave", "atm")), P(None, "atm", "wave"), P("atm", "wave")),
        check_vma=False,
    )
```

```python
import math

import jax
import jax.numpy as jnp
import numpy as np
from jax import lax
from jax.experimental import pallas as pl
from jax.experimental.pallas import tpu as pltpu
from jax.sharding import PartitionSpec as P

ND = 36
NF = 36
K = ND * NF
H = 512
ATM_STEPS = 4
TW = 256
CH = 144
NCH = K // CH
HALF = 72
HALO_ROWS = K + 16
F32 = jnp.float32
BF16 = jnp.bfloat16
I32 = jnp.int32

S_TILES = (0, 1, 2, 4, 5, 6)
N_TILES = (2, 3, 4, 6, 7, 8)
PICK = 8 * len(S_TILES)


def row_tables():
    r = np.arange(HALF)
    d = r % ND
    angle = (d + 0.5) * (2.0 * math.pi / ND)
    up = np.power(1.1, r // ND)
    cosine, sine = np.cos(angle), np.sin(angle)
    reach = 0.7 / up
    rows = [
        up * cosine,
        up * sine,
        np.abs(reach * cosine),
        np.abs(reach * sine),
        np.abs(reach * cosine) + np.abs(reach * sine),
        (cosine > 0).astype(np.float64),
        (sine > 0).astype(np.float64),
    ]
    table = np.stack(rows).astype(np.float32)
    return np.ascontiguousarray(np.broadcast_to(table[:, :, None], table.shape + (128,)))


COS_POS = [bool(math.cos((d + 0.5) * 2.0 * math.pi / ND) > 0) for d in range(ND)]


def west_kind(tile):
    signs = {COS_POS[(8 * tile + s) % ND] for s in range(8)}
    return "both" if len(signs) == 2 else ("west" if True in signs else "east")


def iota(shape, dim):
    return lax.broadcasted_iota(I32, shape, dim)


def hot(mask):
    return jnp.where(mask, 1.0, 0.0).astype(BF16)


def contract(a, b, da, db):
    return lax.dot_general(a, b, (((da,), (db,)), ((), ())), preferred_element_type=F32)


def params(megabytes):
    return pltpu.CompilerParams(vmem_limit_bytes=megabytes << 20)


BIG = 52


HERE = pl.BlockSpec(memory_space=pltpu.VMEM)
AWAY = pl.BlockSpec(memory_space=pl.ANY)


def cost(flops, data):
    return pl.CostEstimate(flops=flops, bytes_accessed=data, transcendentals=0)


def prepare_kernel(code_ref, push_ref, s_ref, pts_ref, pusht_ref, to_prev, to_next, rims, sems):
    blocks = push_ref.shape[0]
    points = code_ref.shape[1]
    ends = ((to_prev, 0), (to_next, points - H))
    loads = [
        pltpu.make_async_copy(s_ref.at[:, pl.ds(lo, H)], rims.at[k, pl.ds(0, K), :], sems.at[k])
        for k, (out, lo) in enumerate(ends)
    ]
    for load in loads:
        load.start()
    pusht_ref[...] = push_ref[...].astype(F32).T.astype(I32)
    before = hot(iota((TW, TW), 0) < iota((TW, TW), 1))
    ones = jnp.ones((TW, TW), BF16)
    running = jnp.zeros((blocks, TW), F32)
    for c in range(points // TW):
        cols = slice(c * TW, (c + 1) * TW)
        tile = code_ref[0:1, cols]
        same = iota((blocks, TW), 0) == tile
        onehot = hot(same)
        earlier = contract(onehot, before, 1, 0) + running
        rank = jnp.sum(jnp.where(same, earlier, 0.0), axis=0, keepdims=True)
        running = running + contract(onehot, ones, 1, 0)
        pts_ref[0:1, cols] = tile.astype(F32)
        pts_ref[1:2, cols] = rank
        pts_ref[2:3, cols] = code_ref[1:2, cols].astype(F32)
        pts_ref[3:8, cols] = jnp.zeros((5, TW), F32)
    stores = []
    for k, (out, lo) in enumerate(ends):
        rows = jnp.concatenate([pts_ref[:, lo : lo + H], jnp.zeros((8, H), F32)], axis=0)
        rims[k, K:, :] = rows.astype(BF16)
        loads[k].wait()
        store = pltpu.make_async_copy(rims.at[k], out, sems.at[2 + k])
        store.start()
        stores.append(store)
    for store in stores:
        store.wait()


def prepare(code, push, spectra):
    blocks, capacity = push.shape
    points = code.shape[1]
    return pl.pallas_call(
        prepare_kernel,
        in_specs=[HERE, HERE, AWAY],
        out_specs=[HERE, HERE, AWAY, AWAY],
        out_shape=[
            jax.ShapeDtypeStruct((8, points), F32),
            jax.ShapeDtypeStruct((capacity, blocks), I32),
            jax.ShapeDtypeStruct((HALO_ROWS, H), BF16),
            jax.ShapeDtypeStruct((HALO_ROWS, H), BF16),
        ],
        scratch_shapes=[pltpu.VMEM((2, HALO_ROWS, H), BF16), pltpu.SemaphoreType.DMA((4,))],
        compiler_params=params(BIG),
        cost_estimate=cost(2 * 2 * blocks * TW * points, 4 * HALO_ROWS * H * 2),
        name="prepare",
    )(code, push, spectra)


CUTS = (0, CH, 3 * CH, 6 * CH, K)


def columns(i):
    return pl.ds(pl.multiple_of(i * TW, TW), TW)


def interact_kernel(it_hbm, *refs):
    *sources, wait_ref, out_hbm, mean_ref, it_ref, s_ref, out_ref, sems = refs
    tiles = out_hbm.shape[1] // TW
    each = tiles // len(sources)
    parts = len(CUTS) - 1
    loads = [
        pltpu.make_async_copy(
            sources[i // each].at[pl.ds(0, K), pl.ds(i % each * TW, TW)], s_ref.at[i], sems.at[i]
        )
        for i in range(tiles)
    ]
    pieces = [
        pltpu.make_async_copy(it_hbm.at[pl.ds(a, b - a), :], it_ref.at[pl.ds(a, b - a), :], sems.at[tiles + c])
        for c, (a, b) in enumerate(zip(CUTS[:-1], CUTS[1:]))
    ]

    def store(i):
        return pltpu.make_async_copy(out_ref.at[i], out_hbm.at[:, columns(i)], sems.at[tiles + parts + i])

    def mean_of(i):
        acc = jnp.zeros((HALF, TW), F32)
        for m in range(NCH):
            s = s_ref[i, m * CH : (m + 1) * CH, :].astype(F32)
            acc = acc + (s[:HALF] + s[HALF:])
        mean = jnp.sum(acc, axis=0, keepdims=True) * (1.0 / K)
        mean_ref[:, columns(i)] = jnp.broadcast_to(mean, (mean_ref.shape[0], TW))

    pieces[0].start()
    loads[0].start()
    pieces[1].start()
    loads[0].wait()
    pieces[2].start()
    loads[1].start()
    mean_of(0)
    for c, (a, b) in enumerate(zip(CUTS[:-1], CUTS[1:])):
        pieces[c].wait()
        if c == 0:
            pieces[3].start()
        out_ref[0, a:b, :] = jnp.dot(it_ref[a:b, :], s_ref[0], preferred_element_type=F32).astype(BF16)
    store(0).start()
    for load in loads[2:]:
        load.start()

    def body(i, carry):
        pltpu.make_async_copy(sources[0].at[pl.ds(0, K), pl.ds(0, TW)], s_ref.at[i], sems.at[i]).wait()
        out_ref[i] = jnp.dot(it_ref[...], s_ref[i], preferred_element_type=F32).astype(BF16)
        store(i).start()
        mean_of(i)
        return carry

    lax.fori_loop(1, tiles, body, 0)
    for i in range(tiles):
        store(i).wait()


def interactions(interact, sources, points, wait, name):
    tiles = points // TW
    return pl.pallas_call(
        interact_kernel,
        in_specs=[AWAY] * (len(sources) + 2),
        out_specs=[AWAY, HERE],
        out_shape=[jax.ShapeDtypeStruct((K, points), BF16), jax.ShapeDtypeStruct((8, points), F32)],
        scratch_shapes=[
            pltpu.VMEM((K, K), BF16),
            pltpu.VMEM((tiles, K, TW), BF16),
            pltpu.VMEM((tiles, K, TW), BF16),
            pltpu.SemaphoreType.DMA((2 * tiles + len(CUTS) - 1,)),
        ],
        compiler_params=params(BIG),
        cost_estimate=cost(2 * K * K * points, K * points * 4),
        name=name,
    )(interact, *sources, wait)


def air_kernel(lat_total, mid_ref, left_ref, right_ref, pusht_ref, air_ref, out_ref, slots):
    rows = mid_ref.shape[1]
    lat_dev = rows - 16
    lane = iota((rows, 128), 1)

    def field(i):
        side = jnp.where(lane < 8, right_ref[i], jnp.where(lane >= 120, left_ref[i], 0.0))
        return jnp.concatenate([mid_ref[i], side], axis=1)

    east, north, spread = field(0), field(1), field(2)
    first = lax.axis_index("atm") * lat_dev - 8
    row = (iota((rows, 256), 0) + first).astype(F32)
    turning = 0.05 + 0.1 * row / lat_total

    def laplace(w):
        around = pltpu.roll(w, rows - 1, 0) + pltpu.roll(w, 1, 0) + pltpu.roll(w, 255, 1) + pltpu.roll(w, 1, 1)
        return around - 4.0 * w

    for _ in range(ATM_STEPS):
        e = east + spread * laplace(east) + turning * north
        n = north + spread * laplace(north) - turning * east
        east, north = e, n
    east = east[8 : 8 + lat_dev, :128]
    north = north[8 : 8 + lat_dev, :128]
    air_ref[0] = east
    air_ref[1] = north
    field_t = jnp.concatenate([east.T, north.T], axis=0).astype(BF16)
    capacity, blocks = pusht_ref.shape
    group = 4
    for g in range(capacity // group):
        cells = jnp.concatenate([pusht_ref[g * group + k : g * group + k + 1, :] for k in range(group)], axis=1)
        at_row = hot(iota((lat_dev, group * blocks), 0) == (cells >> 7))
        picked = jnp.dot(field_t, at_row, preferred_element_type=F32)
        at_col = iota((128, group * blocks), 0) == (cells & 127)
        for c in range(2):
            value = jnp.sum(jnp.where(at_col, picked[c * 128 : (c + 1) * 128], 0.0), axis=0, keepdims=True)
            for k in range(group):
                at = c * capacity + g * group + k
                slots[at : at + 1, :] = value[:, k * blocks : (k + 1) * blocks]
    own = slots[...]
    stacked = jnp.concatenate([pltpu.roll(own, 1, 1), own, pltpu.roll(own, blocks - 1, 1), jnp.zeros_like(own)], axis=0)
    out_ref[...] = stacked.T.reshape(out_ref.shape)


def air(lat_total, mid, left, right, pusht):
    capacity, blocks = pusht.shape
    lat_dev = mid.shape[1] - 16
    assert mid.shape[2] == 128 and blocks == 128
    return pl.pallas_call(
        lambda *refs: air_kernel(lat_total, *refs),
        in_specs=[HERE] * 4,
        out_specs=[HERE] * 2,
        out_shape=[
            jax.ShapeDtypeStruct((2, lat_dev, 128), F32),
            jax.ShapeDtypeStruct((blocks, 1, 8 * capacity), F32),
        ],
        scratch_shapes=[pltpu.VMEM((2 * capacity, blocks), F32)],
        compiler_params=params(BIG),
        cost_estimate=cost(2 * 256 * lat_dev * capacity * blocks, 600000),
        name="air",
    )(mid, left, right, pusht)


def winds_at(table, tile, rank):
    slots = table.shape[0] // 2
    tiles = table.shape[1]
    points = tile.shape[1]
    onehot = hot(iota((tiles, points), 0) == tile.astype(I32))
    values = jnp.dot(table, onehot, preferred_element_type=F32)
    at = iota((slots, points), 0) == rank.astype(I32)
    east = jnp.sum(jnp.where(at, values[:slots], 0.0), axis=0, keepdims=True)
    north = jnp.sum(jnp.where(at, values[slots:], 0.0), axis=0, keepdims=True)
    return east, north, onehot, at


def growth_pattern(tab_ref, east, north):
    return tab_ref[0] * (0.2 * east) + tab_ref[1] * (0.2 * north)


def step_scale(m, h):
    return 1.1 ** (4 * m + 2 * h - NF / 2)


SW = 512


def lane_tile(i):
    return pl.ds(pl.multiple_of(i * 128, 128), 128)


def stress_kernel(
    tab_ref, got_ref, p_ref, s_hbm, wait_ref, send_ref, winds_ref, s_ref, table, waves, sems
):
    points = p_ref.shape[1]
    blocks = got_ref.shape[0]
    slots = got_ref.shape[2] // 4
    groups = points // SW
    loads = [
        pltpu.make_async_copy(s_hbm.at[:, pl.ds(g * SW, SW)], s_ref.at[:, pl.ds(g * SW, SW)], sems.at[g])
        for g in range(groups)
    ]
    for load in loads[:2]:
        load.start()
    table[...] = got_ref[...].reshape(blocks, got_ref.shape[2]).T.astype(BF16)
    winds_ref[3:8, :] = jnp.zeros((5, winds_ref.shape[1]), F32)

    for g in range(groups):
        cols = slice(g * SW, (g + 1) * SW)
        east, north, _, _ = winds_at(table[slots : 2 * slots, :], p_ref[0:1, cols], p_ref[1:2, cols])
        mask = p_ref[2:3, cols]
        winds_ref[0:1, cols] = east * mask
        winds_ref[1:2, cols] = north * mask
        winds_ref[2:3, cols] = mask

    def tile(i, carry):
        at = lane_tile(i)
        pattern = growth_pattern(tab_ref, winds_ref[0:1, at], winds_ref[1:2, at])
        acc = jnp.zeros((HALF, 128), F32)
        for m in range(NCH):
            s = s_ref[m * CH : (m + 1) * CH, lane_tile(i)].astype(F32)
            for h in range(2):
                scale = step_scale(m, h)
                bent = jnp.maximum((scale * scale) * pattern - 0.25 * scale, 0.0)
                acc = acc + bent * s[h * HALF : (h + 1) * HALF]
        waves[0:1, lane_tile(i)] = jnp.sum(acc * tab_ref[0], axis=0, keepdims=True)
        waves[1:2, lane_tile(i)] = jnp.sum(acc * tab_ref[1], axis=0, keepdims=True)
        return carry

    per = SW // 128
    for g in range(groups):
        loads[g].wait()
        if g + 2 < groups:
            loads[g + 2].start()
        lax.fori_loop(g * per, (g + 1) * per, tile, 0)

    total = jnp.zeros((blocks, 2 * slots), F32)
    for g in range(groups):
        cols = slice(g * SW, (g + 1) * SW)
        east, north, mask = (winds_ref[k : k + 1, cols] for k in range(3))
        speed = jnp.sqrt(east * east + north * north + 0.25)
        stress_x = 0.3 * speed * east + mask * (waves[0:1, cols] * (0.4 / K))
        stress_y = 0.3 * speed * north + mask * (waves[1:2, cols] * (0.4 / K))
        rough = mask * 0.2 * jnp.sqrt(stress_x * stress_x + stress_y * stress_y + 0.01)
        onehot = hot(iota((blocks, SW), 0) == p_ref[0:1, cols].astype(I32))
        at = iota((slots // 2, SW), 0) == p_ref[1:2, cols].astype(I32)
        values = jnp.concatenate([jnp.where(at, v, 0.0) for v in (stress_x, stress_y, rough, mask)], axis=0)
        high = values.astype(BF16)
        rest = values - high.astype(F32)
        middle = rest.astype(BF16)
        low = (rest - middle.astype(F32)).astype(BF16)
        total = total + contract(
            jnp.concatenate([onehot] * 3, axis=1), jnp.concatenate([high, middle, low], axis=1), 1, 1
        )
    send_ref[...] = total.reshape(send_ref.shape)


def stresses(tab, got, pts, spectra, wait):
    points = spectra.shape[1]
    blocks = got.shape[0]
    capacity = got.shape[2] // 8
    return pl.pallas_call(
        stress_kernel,
        in_specs=[HERE] * 3 + [AWAY] * 2,
        out_specs=[HERE] * 2,
        out_shape=[
            jax.ShapeDtypeStruct((blocks, 1, 4 * capacity), F32),
            jax.ShapeDtypeStruct((8, points), F32),
        ],
        scratch_shapes=[
            pltpu.VMEM((K, points), BF16),
            pltpu.VMEM((8 * capacity, blocks), BF16),
            pltpu.VMEM((8, points), F32),
            pltpu.SemaphoreType.DMA((points // SW,)),
        ],
        compiler_params=params(BIG),
        cost_estimate=cost(10 * K * points, K * points * 2),
        name="stress",
    )(tab, got, pts, spectra, wait)


def chosen_rows(x, tiles):
    rows = [x[HALF * h + 8 * t : HALF * h + 8 * t + 8] for h in range(2) for t in tiles]
    return jnp.concatenate(rows, axis=0).astype(BF16)


def move_kernel(
    tab_ref, winds_ref, link_ref, got_ref, mean_ref, it_hbm, s_hbm, sb_hbm, sa_hbm, n_hbm,
    out_hbm, token, table, rim, rim_winds, it_ref, s_ref, n_ref, product, natural, south, north, staged, hots, south_y, north_y, flows, sems,
):
    points = link_ref.shape[1]
    parts = points // H + 2
    loads = []
    for g in range(parts):
        to = pl.ds(g * H, H)
        if g == 0:
            source = sb_hbm.at[pl.ds(0, K), :]
        elif g == parts - 1:
            source = sa_hbm.at[pl.ds(0, K), :]
        else:
            source = s_hbm.at[:, pl.ds((g - 1) * H, H)]
        loads.append(pltpu.make_async_copy(source, s_ref.at[:, to], sems.at[g]))
    matrix = pltpu.make_async_copy(it_hbm, it_ref, sems.at[parts])
    products = [
        pltpu.make_async_copy(n_hbm.at[:, pl.ds(g * H, H)], n_ref.at[:, pl.ds(g * H, H)], sems.at[parts + 3 + g])
        for g in range(parts - 2)
    ]
    places = [
        pltpu.make_async_copy(ref.at[pl.ds(K, 16), :], rim.at[k], sems.at[parts + 1 + k])
        for k, ref in enumerate((sb_hbm, sa_hbm))
    ]
    for place in places:
        place.start()

    order = (1, 0, *range(2, parts))

    def start_part(k):
        if k < parts:
            loads[order[k]].start()
            if 0 < order[k] < parts - 1:
                products[order[k] - 1].start()

    start_part(0)
    token[...] = jnp.zeros_like(token)
    width = TW + H

    def build(j, carry):
        mine = pl.ds(pl.multiple_of(j * TW, TW), TW)
        hots[j, 0] = hot(iota((width, TW), 0) == link_ref[2:3, mine] - j * TW)
        hots[j, 1] = hot(iota((width, TW), 0) == link_ref[3:4, mine] - (j * TW + H))
        return carry

    table[...] = got_ref[...].reshape(got_ref.shape[0], got_ref.shape[2]).T.astype(BF16)
    slots = table.shape[0] // 4
    for k in range(2):
        places[k].wait()
        pts = rim[k].astype(F32)
        east, north_, _, _ = winds_at(table[2 * k * slots : (2 * k + 1) * slots, :], pts[0:1], pts[1:2])
        rim_winds[0:1, k * H : (k + 1) * H] = east * pts[2:3]
        rim_winds[1:2, k * H : (k + 1) * H] = north_ * pts[2:3]
        rim_winds[2:3, k * H : (k + 1) * H] = pts[2:3]
    middle = points // TW // 2
    lax.fori_loop(0, middle, build, 0)
    start_part(1)
    matrix.start()
    lax.fori_loop(middle, points // TW, build, 0)
    low = iota((8, 128), 0) < 4

    def fill(i, lanes, mean, kinds):
        at = lane_tile(i)
        if kinds == "sn":
            air, over = winds_ref, lane_tile(i - per)
        else:
            air, over = rim_winds, at if kinds == "s" else lane_tile(i - points // 128)
        pattern = growth_pattern(tab_ref, air[0:1, over], air[1:2, over])
        msk = jnp.broadcast_to(air[2:3, over], (8, 128))
        quota = (0.15 * msk) * jnp.broadcast_to(mean / (1.0 + mean), (8, 128))
        wet = 0.5 * msk
        for m in range(NCH):
            rows = slice(m * CH, (m + 1) * CH)
            s = s_ref[rows, at].astype(F32)
            n = n_ref[rows, lane_tile(i - per)].astype(F32) if kinds == "sn" else product[rows, lanes]
            out = []
            for h in range(2):
                scale = step_scale(m, h)
                power = 1.21 ** (4 * m + 2 * h - NF / 2)
                near = msk - power * quota
                far = msk - (1.21 * power) * quota
                keeps = [near] * 4 + [jnp.where(low, near, far)] + [far] * 4
                for t, keep in enumerate(keeps):
                    tr = slice(8 * t, 8 * t + 8)
                    k = slice(HALF * h + 8 * t, HALF * h + 8 * t + 8)
                    grow = jnp.maximum(scale * pattern[tr] - 0.25, 0.0)
                    out.append(s[k] * (keep + grow) + n[k] * wet)
            x = jnp.concatenate(out, axis=0)
            natural[rows, at] = x.astype(BF16)
            picks = slice(m * 2 * PICK, (m + 1) * 2 * PICK)
            if "s" in kinds:
                south[picks, at] = chosen_rows(x, S_TILES)
            if "n" in kinds:
                north[picks, lane_tile(i - H // 128)] = chosen_rows(x, N_TILES)

    per = H // 128

    def fill_part(g, kinds):
        def own(i, carry):
            fill(i, slice(0, 128), mean_ref[0:1, lane_tile(i - per)], kinds)
            return carry

        if kinds == "sn":
            lax.fori_loop(g * per, (g + 1) * per, own, 0)
            return

        def body(q, carry):
            cols = pl.ds(pl.multiple_of(q * TW, TW), TW)
            product[...] = jnp.dot(it_ref[...], s_ref[:, cols], preferred_element_type=F32)
            acc = jnp.zeros((HALF, TW), F32)
            for m in range(NCH):
                s = s_ref[m * CH : (m + 1) * CH, cols].astype(F32)
                acc = acc + (s[:HALF] + s[HALF:])
            mean = jnp.sum(acc, axis=0, keepdims=True) * (1.0 / K)
            for l in range(TW // 128):
                lanes = slice(l * 128, (l + 1) * 128)
                fill(q * (TW // 128) + l, lanes, mean[:, lanes], kinds)
            return carry

        lax.fori_loop(g * (H // TW), (g + 1) * (H // TW), body, 0)

    def wait_part(k):
        loads[order[k]].wait()
        if 0 < order[k] < parts - 1:
            products[order[k] - 1].wait()
        start_part(k + 2)

    def output(j):
        window = pl.ds(pl.multiple_of(j * TW, TW), width)
        south_y[...] = jnp.dot(south[:, window], hots[j, 0], preferred_element_type=F32)
        north_y[...] = jnp.dot(north[:, window], hots[j, 1], preferred_element_type=F32)
        first = j * (TW // 128) + per
        for l in range(TW // 128):
            msk = winds_ref[2:3, lane_tile(first - per + l)]
            flows[l, 0] = tab_ref[2] * msk
            flows[l, 1] = tab_ref[3] * msk
        lane = iota((8, 128), 1)
        count = TW // 128
        for m in range(NCH):
            rows = slice(m * CH, (m + 1) * CH)
            near = [natural[rows, lane_tile(first + o - 1)].astype(F32) for o in range(count + 2)]
            ys = south_y[m * 2 * PICK : (m + 1) * 2 * PICK, :]
            yn = north_y[m * 2 * PICK : (m + 1) * 2 * PICK, :]
            out = [[] for _ in range(count)]
            for h in range(2):
                shrink = 1.1 ** (-(4 * m + 2 * h))
                for t in range(9):
                    at = slice(HALF * h + 8 * t, HALF * h + 8 * t + 8)
                    tr = slice(8 * t, 8 * t + 8)
                    kind = west_kind(t)
                    tile = [n[at] for n in near]
                    if kind != "east":
                        ahead = [pltpu.roll(x, 1, 1) for x in tile[:-1]]
                    if kind != "west":
                        behind = [pltpu.roll(x, 127, 1) for x in tile[1:]]
                    for l in range(count):
                        c = tile[l + 1]
                        if kind != "east":
                            x = west = jnp.where(lane == 0, ahead[l], ahead[l + 1])
                        if kind != "west":
                            x = east = jnp.where(lane == 127, behind[l + 1], behind[l])
                        if kind == "both":
                            x = jnp.where(tab_ref[5, tr] > 0, west, east)
                        lanes = slice(l * 128, (l + 1) * 128)
                        if t in S_TILES:
                            k = PICK * h + 8 * S_TILES.index(t)
                            y = ys[k : k + 8, lanes]
                        if t in N_TILES:
                            k = PICK * h + 8 * N_TILES.index(t)
                            z = yn[k : k + 8, lanes]
                            y = jnp.where(tab_ref[6, tr] > 0, y, z) if t in S_TILES else z
                        flow = flows[l, 0, tr] * x + flows[l, 1, tr] * y - tab_ref[4, tr] * c
                        out[l].append(c + shrink * flow)
            for l in range(count):
                staged[rows, lane_tile(j * count + l)] = jnp.concatenate(out[l], axis=0).astype(BF16)

    def stores(j):
        at = pl.ds(j * TW, TW)
        return pltpu.make_async_copy(staged.at[:, at], out_hbm.at[:, at], sems.at[2 * parts + 1 + j])

    pair = H // TW
    wait_part(0)
    fill_part(1, "sn")
    wait_part(1)
    matrix.wait()
    fill_part(0, "s")
    for g in range(2, parts):
        wait_part(g)
        fill_part(g, "n" if g == parts - 1 else "sn")
        lax.fori_loop((g - 2) * pair, (g - 1) * pair, lambda j, c: (output(j), c)[1], 0)
        for j in range((g - 2) * pair, (g - 1) * pair):
            stores(j).start()
    for j in range(points // TW):
        stores(j).wait()


def move(tab, winds, links, got, mean, interact, spectra, before, after, nonlinear):
    points = links.shape[1]
    extended = points + 2 * H
    return pl.pallas_call(
        move_kernel,
        in_specs=[HERE] * 5 + [AWAY] * 5,
        out_specs=[AWAY, HERE],
        out_shape=[jax.ShapeDtypeStruct((K, points), BF16), jax.ShapeDtypeStruct((8, 128), F32)],
        scratch_shapes=[
            pltpu.VMEM((got.shape[2], got.shape[0]), BF16),
            pltpu.VMEM((2, 16, H), BF16),
            pltpu.VMEM((8, 2 * H), F32),
            pltpu.VMEM((K, K), BF16),
            pltpu.VMEM((K, extended), BF16),
            pltpu.VMEM((K, points), BF16),
            pltpu.VMEM((K, TW), F32),
            pltpu.VMEM((K, extended), BF16),
            pltpu.VMEM((18 * PICK, points + H), BF16),
            pltpu.VMEM((18 * PICK, points + H), BF16),
            pltpu.VMEM((K, points), BF16),
            pltpu.VMEM((points // TW, 2, TW + H, TW), BF16),
            pltpu.VMEM((18 * PICK, TW), F32),
            pltpu.VMEM((18 * PICK, TW), F32),
            pltpu.VMEM((TW // 128, 2, HALF, 128), F32),
            pltpu.SemaphoreType.DMA((2 * (points // H + 2) + 1 + points // TW,)),
        ],
        compiler_params=params(BIG),
        cost_estimate=cost(2 * 2 * 18 * PICK * (TW + H) * points + 2 * K * K * extended, K * points * 8),
        name="move",
    )(tab, winds, links, got, mean, interact, spectra, before, after, nonlinear)


def cell_kernel(got_ref, push_ref, pusht_ref, air_ref, wait_ref, wind_ref, rough_ref, left, right):
    capacity, blocks = pusht_ref.shape
    lat_dev = air_ref.shape[1]
    values = got_ref[...].reshape(blocks, 4 * capacity).T
    high = values.astype(BF16).astype(F32)
    low = values - high
    for r in range(capacity):
        cols = slice(r * blocks, (r + 1) * blocks)
        at_row = iota((lat_dev, blocks), 0) == (pusht_ref[r : r + 1, :] >> 7)
        for part, source in enumerate((high, low)):
            rows = [
                jnp.where(at_row, source[c * capacity + r : c * capacity + r + 1, :], 0.0) for c in range(4)
            ]
            left[part * 4 * lat_dev : (part + 1) * 4 * lat_dev, cols] = jnp.concatenate(rows, axis=0).astype(BF16)
        right[cols, :] = hot(iota((blocks, 128), 1) == (push_ref[:, r : r + 1] & 127))
    sums = jnp.dot(left[...], right[...], preferred_element_type=F32)
    sums = sums[: 4 * lat_dev] + sums[4 * lat_dev :]
    sx, sy, rough, share = (sums[c * lat_dev : (c + 1) * lat_dev] for c in range(4))
    count = jnp.maximum(share, 1.0)
    wind_ref[0] = air_ref[0] - 0.5 * (sx / count)
    wind_ref[1] = air_ref[1] - 0.5 * (sy / count)
    rough_ref[...] = rough / count


def cells(got, push, pusht, air_state, wait):
    capacity, blocks = pusht.shape
    lat_dev = air_state.shape[1]
    return pl.pallas_call(
        cell_kernel,
        in_specs=[HERE] * 4 + [AWAY],
        out_specs=[HERE] * 2,
        out_shape=[
            jax.ShapeDtypeStruct(air_state.shape, F32),
            jax.ShapeDtypeStruct(air_state.shape[1:], F32),
        ],
        scratch_shapes=[
            pltpu.VMEM((8 * lat_dev, capacity * blocks), BF16),
            pltpu.VMEM((capacity * blocks, 128), BF16),
        ],
        compiler_params=params(BIG),
        cost_estimate=cost(2 * 8 * lat_dev * 128 * capacity * blocks, 400000),
        name="cells",
    )(got, push, pusht, air_state, wait)


def chain(axis, step):
    peers = lax.axis_size(axis)
    pairs = [(i, i + 1) for i in range(peers - 1)]
    return pairs if step > 0 else [(j, i) for i, j in pairs]


def shards(spectra, interact, sea_mask, sea_tile, push_list, neighbors, air_wind, diffusion):
    both = ("wave", "atm")
    tab = jnp.asarray(row_tables())
    lat_total = air_wind.shape[1] * lax.axis_size("atm")
    points = spectra.shape[1]
    push = push_list[0]

    pack = jnp.concatenate([air_wind, diffusion[None]], axis=0)
    above = lax.ppermute(pack[:, -8:], "atm", chain("atm", 1))
    below = lax.ppermute(pack[:, :8], "atm", chain("atm", -1))
    mid = jnp.concatenate([above, pack, below], axis=1)
    pts, pusht, to_prev, to_next = prepare(jnp.stack([sea_tile, sea_mask]), push, spectra)
    mid, pts, pusht, to_prev, to_next = lax.optimization_barrier((mid, pts, pusht, to_prev, to_next))
    left = lax.ppermute(mid, "wave", chain("wave", 1))
    right = lax.ppermute(mid, "wave", chain("wave", -1))


    air_state, outgoing = air(lat_total, mid, left, right, pusht)
    outgoing, to_prev, to_next = lax.optimization_barrier((outgoing, to_prev, to_next))
    arrived = lax.all_to_all(outgoing, both, split_axis=0, concat_axis=0, tiled=True)
    before = lax.ppermute(to_next, both, chain(both, 1))
    after = lax.ppermute(to_prev, both, chain(both, -1))
    nonlinear, mean = interactions(interact, [spectra], points, outgoing, "interact_own")
    outbound, winds = stresses(tab, arrived, pts, spectra, mean)
    inbound = lax.all_to_all(outbound, both, split_axis=0, concat_axis=0, tiled=True)
    wave_spectra, token = move(tab, winds, neighbors, arrived, mean, interact, spectra, before, after, nonlinear)
    surface_wind, roughness = cells(inbound, push, pusht, air_state, token)
    return (wave_spectra, surface_wind, roughness)


def solution(mesh):
    placed = (
        P(None, ("wave", "atm")),
        P(),
        P(("wave", "atm")),
        P(("wave", "atm")),
        P(("wave", "atm"), None, None),
        P(None, ("wave", "atm")),
        P(None, "atm", "wave"),
        P("atm", "wave"),
    )
    return jax.shard_map(
        shards,
        mesh=mesh,
        in_specs=placed,
        out_specs=(P(None, ("wave", "atm")), P(None, "atm", "wave"), P("atm", "wave")),
        check_vma=False,
    )
```

```python
import math

import jax
import jax.numpy as jnp
import numpy as np
from jax import lax
from jax.experimental import pallas as pl
from jax.experimental.pallas import tpu as pltpu
from jax.sharding import PartitionSpec as P

ND = 36
NF = 36
K = ND * NF
H = 512
ATM_STEPS = 4
TW = 256
CH = 144
NCH = K // CH
HALF = 72
HALO_ROWS = K + 16
F32 = jnp.float32
BF16 = jnp.bfloat16
I32 = jnp.int32

S_TILES = (0, 1, 2, 4, 5, 6)
N_TILES = (2, 3, 4, 6, 7, 8)
PICK = 8 * len(S_TILES)


def row_tables():
    r = np.arange(HALF)
    d = r % ND
    angle = (d + 0.5) * (2.0 * math.pi / ND)
    up = np.power(1.1, r // ND)
    cosine, sine = np.cos(angle), np.sin(angle)
    reach = 0.7 / up
    rows = [
        up * cosine,
        up * sine,
        np.abs(reach * cosine),
        np.abs(reach * sine),
        np.abs(reach * cosine) + np.abs(reach * sine),
        (cosine > 0).astype(np.float64),
        (sine > 0).astype(np.float64),
    ]
    table = np.stack(rows).astype(np.float32)
    return np.ascontiguousarray(np.broadcast_to(table[:, :, None], table.shape + (128,)))


COS_POS = [bool(math.cos((d + 0.5) * 2.0 * math.pi / ND) > 0) for d in range(ND)]


def west_kind(tile):
    signs = {COS_POS[(8 * tile + s) % ND] for s in range(8)}
    return "both" if len(signs) == 2 else ("west" if True in signs else "east")


def iota(shape, dim):
    return lax.broadcasted_iota(I32, shape, dim)


def hot(mask):
    return jnp.where(mask, 1.0, 0.0).astype(BF16)


def contract(a, b, da, db):
    return lax.dot_general(a, b, (((da,), (db,)), ((), ())), preferred_element_type=F32)


def params(megabytes):
    return pltpu.CompilerParams(vmem_limit_bytes=megabytes << 20)


BIG = 52


HERE = pl.BlockSpec(memory_space=pltpu.VMEM)
AWAY = pl.BlockSpec(memory_space=pl.ANY)


def cost(flops, data):
    return pl.CostEstimate(flops=flops, bytes_accessed=data, transcendentals=0)


def prepare_kernel(code_ref, push_ref, s_ref, pts_ref, pusht_ref, to_prev, to_next, rims, sems):
    blocks = push_ref.shape[0]
    points = code_ref.shape[1]
    ends = ((to_prev, 0), (to_next, points - H))
    loads = [
        pltpu.make_async_copy(s_ref.at[:, pl.ds(lo, H)], rims.at[k, pl.ds(0, K), :], sems.at[k])
        for k, (out, lo) in enumerate(ends)
    ]
    for load in loads:
        load.start()
    pusht_ref[...] = push_ref[...].astype(F32).T.astype(I32)
    before = hot(iota((TW, TW), 0) < iota((TW, TW), 1))
    ones = jnp.ones((TW, TW), BF16)
    running = jnp.zeros((blocks, TW), F32)
    for c in range(points // TW):
        cols = slice(c * TW, (c + 1) * TW)
        tile = code_ref[0:1, cols]
        same = iota((blocks, TW), 0) == tile
        onehot = hot(same)
        earlier = contract(onehot, before, 1, 0) + running
        rank = jnp.sum(jnp.where(same, earlier, 0.0), axis=0, keepdims=True)
        running = running + contract(onehot, ones, 1, 0)
        pts_ref[0:1, cols] = tile.astype(F32)
        pts_ref[1:2, cols] = rank
        pts_ref[2:3, cols] = code_ref[1:2, cols].astype(F32)
        pts_ref[3:8, cols] = jnp.zeros((5, TW), F32)
    stores = []
    for k, (out, lo) in enumerate(ends):
        rows = jnp.concatenate([pts_ref[:, lo : lo + H], jnp.zeros((8, H), F32)], axis=0)
        rims[k, K:, :] = rows.astype(BF16)
        loads[k].wait()
        store = pltpu.make_async_copy(rims.at[k], out, sems.at[2 + k])
        store.start()
        stores.append(store)
    for store in stores:
        store.wait()


def prepare(code, push, spectra):
    blocks, capacity = push.shape
    points = code.shape[1]
    return pl.pallas_call(
        prepare_kernel,
        in_specs=[HERE, HERE, AWAY],
        out_specs=[HERE, HERE, AWAY, AWAY],
        out_shape=[
            jax.ShapeDtypeStruct((8, points), F32),
            jax.ShapeDtypeStruct((capacity, blocks), I32),
            jax.ShapeDtypeStruct((HALO_ROWS, H), BF16),
            jax.ShapeDtypeStruct((HALO_ROWS, H), BF16),
        ],
        scratch_shapes=[pltpu.VMEM((2, HALO_ROWS, H), BF16), pltpu.SemaphoreType.DMA((4,))],
        compiler_params=params(BIG),
        cost_estimate=cost(2 * 2 * blocks * TW * points, 4 * HALO_ROWS * H * 2),
        name="prepare",
    )(code, push, spectra)


CUTS = (0, CH, 3 * CH, 6 * CH, K)


def columns(i):
    return pl.ds(pl.multiple_of(i * TW, TW), TW)


def interact_kernel(it_hbm, *refs):
    *sources, wait_ref, out_hbm, mean_ref, it_ref, s_ref, out_ref, sems = refs
    tiles = out_hbm.shape[1] // TW
    each = tiles // len(sources)
    parts = len(CUTS) - 1
    loads = [
        pltpu.make_async_copy(
            sources[i // each].at[pl.ds(0, K), pl.ds(i % each * TW, TW)], s_ref.at[i], sems.at[i]
        )
        for i in range(tiles)
    ]
    pieces = [
        pltpu.make_async_copy(it_hbm.at[pl.ds(a, b - a), :], it_ref.at[pl.ds(a, b - a), :], sems.at[tiles + c])
        for c, (a, b) in enumerate(zip(CUTS[:-1], CUTS[1:]))
    ]

    def store(i):
        return pltpu.make_async_copy(out_ref.at[i], out_hbm.at[:, columns(i)], sems.at[tiles + parts + i])

    def load_at(i):
        return pltpu.make_async_copy(sources[0].at[pl.ds(0, K), columns(i)], s_ref.at[i], sems.at[i])

    def mean_of(i):
        acc = jnp.zeros((HALF, TW), F32)
        for m in range(NCH):
            s = s_ref[i, m * CH : (m + 1) * CH, :].astype(F32)
            acc = acc + (s[:HALF] + s[HALF:])
        mean = jnp.sum(acc, axis=0, keepdims=True) * (1.0 / K)
        mean_ref[:, columns(i)] = jnp.broadcast_to(mean, (mean_ref.shape[0], TW))

    pieces[0].start()
    loads[0].start()
    pieces[1].start()
    loads[0].wait()
    pieces[2].start()
    loads[1].start()
    mean_of(0)
    for c, (a, b) in enumerate(zip(CUTS[:-1], CUTS[1:])):
        pieces[c].wait()
        if c == 0:
            pieces[3].start()
            load_at(2).start()
        out_ref[0, a:b, :] = jnp.dot(it_ref[a:b, :], s_ref[0], preferred_element_type=F32).astype(BF16)
    store(0).start()

    def body(i, carry):
        @pl.when(i + 2 < tiles)
        def _():
            load_at(i + 2).start()

        load_at(i).wait()
        out_ref[i] = jnp.dot(it_ref[...], s_ref[i], preferred_element_type=F32).astype(BF16)
        store(i).start()
        mean_of(i)
        return carry

    lax.fori_loop(1, tiles, body, 0)
    for i in range(tiles):
        store(i).wait()


def interactions(interact, sources, points, wait, name):
    tiles = points // TW
    return pl.pallas_call(
        interact_kernel,
        in_specs=[AWAY] * (len(sources) + 2),
        out_specs=[AWAY, HERE],
        out_shape=[jax.ShapeDtypeStruct((K, points), BF16), jax.ShapeDtypeStruct((8, points), F32)],
        scratch_shapes=[
            pltpu.VMEM((K, K), BF16),
            pltpu.VMEM((tiles, K, TW), BF16),
            pltpu.VMEM((tiles, K, TW), BF16),
            pltpu.SemaphoreType.DMA((2 * tiles + len(CUTS) - 1,)),
        ],
        compiler_params=params(BIG),
        cost_estimate=cost(2 * K * K * points, K * points * 4),
        name=name,
    )(interact, *sources, wait)


def air_kernel(lat_total, mid_ref, left_ref, right_ref, pusht_ref, air_ref, out_ref, slots):
    rows = mid_ref.shape[1]
    lat_dev = rows - 16
    lane = iota((rows, 128), 1)

    def field(i):
        side = jnp.where(lane < 8, right_ref[i], jnp.where(lane >= 120, left_ref[i], 0.0))
        return jnp.concatenate([mid_ref[i], side], axis=1)

    east, north, spread = field(0), field(1), field(2)
    first = lax.axis_index("atm") * lat_dev - 8
    row = (iota((rows, 256), 0) + first).astype(F32)
    turning = 0.05 + 0.1 * row / lat_total

    def laplace(w):
        around = pltpu.roll(w, rows - 1, 0) + pltpu.roll(w, 1, 0) + pltpu.roll(w, 255, 1) + pltpu.roll(w, 1, 1)
        return around - 4.0 * w

    for _ in range(ATM_STEPS):
        e = east + spread * laplace(east) + turning * north
        n = north + spread * laplace(north) - turning * east
        east, north = e, n
    east = east[8 : 8 + lat_dev, :128]
    north = north[8 : 8 + lat_dev, :128]
    air_ref[0] = east
    air_ref[1] = north
    field_t = jnp.concatenate([east.T, north.T], axis=0).astype(BF16)
    capacity, blocks = pusht_ref.shape
    group = 4
    for g in range(capacity // group):
        cells = jnp.concatenate([pusht_ref[g * group + k : g * group + k + 1, :] for k in range(group)], axis=1)
        at_row = hot(iota((lat_dev, group * blocks), 0) == (cells >> 7))
        picked = jnp.dot(field_t, at_row, preferred_element_type=F32)
        at_col = iota((128, group * blocks), 0) == (cells & 127)
        for c in range(2):
            value = jnp.sum(jnp.where(at_col, picked[c * 128 : (c + 1) * 128], 0.0), axis=0, keepdims=True)
            for k in range(group):
                at = c * capacity + g * group + k
                slots[at : at + 1, :] = value[:, k * blocks : (k + 1) * blocks]
    own = slots[...]
    stacked = jnp.concatenate([pltpu.roll(own, 1, 1), own, pltpu.roll(own, blocks - 1, 1), jnp.zeros_like(own)], axis=0)
    out_ref[...] = stacked.T.reshape(out_ref.shape)


def air(lat_total, mid, left, right, pusht):
    capacity, blocks = pusht.shape
    lat_dev = mid.shape[1] - 16
    assert mid.shape[2] == 128 and blocks == 128
    return pl.pallas_call(
        lambda *refs: air_kernel(lat_total, *refs),
        in_specs=[HERE] * 4,
        out_specs=[HERE] * 2,
        out_shape=[
            jax.ShapeDtypeStruct((2, lat_dev, 128), F32),
            jax.ShapeDtypeStruct((blocks, 1, 8 * capacity), F32),
        ],
        scratch_shapes=[pltpu.VMEM((2 * capacity, blocks), F32)],
        compiler_params=params(BIG),
        cost_estimate=cost(2 * 256 * lat_dev * capacity * blocks, 600000),
        name="air",
    )(mid, left, right, pusht)


def winds_at(table, tile, rank):
    slots = table.shape[0] // 2
    tiles = table.shape[1]
    points = tile.shape[1]
    onehot = hot(iota((tiles, points), 0) == tile.astype(I32))
    values = jnp.dot(table, onehot, preferred_element_type=F32)
    at = iota((slots, points), 0) == rank.astype(I32)
    east = jnp.sum(jnp.where(at, values[:slots], 0.0), axis=0, keepdims=True)
    north = jnp.sum(jnp.where(at, values[slots:], 0.0), axis=0, keepdims=True)
    return east, north, onehot, at


def growth_pattern(tab_ref, east, north):
    return tab_ref[0] * (0.2 * east) + tab_ref[1] * (0.2 * north)


def step_scale(m, h):
    return 1.1 ** (4 * m + 2 * h - NF / 2)


SW = 512


def lane_tile(i):
    return pl.ds(pl.multiple_of(i * 128, 128), 128)


def stress_kernel(
    tab_ref, got_ref, p_ref, s_hbm, wait_ref, send_ref, winds_ref, s_ref, table, waves, sems
):
    points = p_ref.shape[1]
    blocks = got_ref.shape[0]
    slots = got_ref.shape[2] // 4
    groups = points // SW
    loads = [
        pltpu.make_async_copy(s_hbm.at[:, pl.ds(g * SW, SW)], s_ref.at[:, pl.ds(g * SW, SW)], sems.at[g])
        for g in range(groups)
    ]
    for load in loads[:2]:
        load.start()
    table[...] = got_ref[...].reshape(blocks, got_ref.shape[2]).T.astype(BF16)
    winds_ref[3:8, :] = jnp.zeros((5, winds_ref.shape[1]), F32)

    for g in range(groups):
        cols = slice(g * SW, (g + 1) * SW)
        east, north, _, _ = winds_at(table[slots : 2 * slots, :], p_ref[0:1, cols], p_ref[1:2, cols])
        mask = p_ref[2:3, cols]
        winds_ref[0:1, cols] = east * mask
        winds_ref[1:2, cols] = north * mask
        winds_ref[2:3, cols] = mask

    def tile(i, carry):
        at = lane_tile(i)
        pattern = growth_pattern(tab_ref, winds_ref[0:1, at], winds_ref[1:2, at])
        acc = jnp.zeros((HALF, 128), F32)
        for m in range(NCH):
            s = s_ref[m * CH : (m + 1) * CH, lane_tile(i)].astype(F32)
            for h in range(2):
                scale = step_scale(m, h)
                bent = jnp.maximum((scale * scale) * pattern - 0.25 * scale, 0.0)
                acc = acc + bent * s[h * HALF : (h + 1) * HALF]
        waves[0:1, lane_tile(i)] = jnp.sum(acc * tab_ref[0], axis=0, keepdims=True)
        waves[1:2, lane_tile(i)] = jnp.sum(acc * tab_ref[1], axis=0, keepdims=True)
        return carry

    per = SW // 128
    for g in range(groups):
        loads[g].wait()
        if g + 2 < groups:
            loads[g + 2].start()
        lax.fori_loop(g * per, (g + 1) * per, tile, 0)

    total = jnp.zeros((blocks, 2 * slots), F32)
    for g in range(groups):
        cols = slice(g * SW, (g + 1) * SW)
        east, north, mask = (winds_ref[k : k + 1, cols] for k in range(3))
        speed = jnp.sqrt(east * east + north * north + 0.25)
        stress_x = 0.3 * speed * east + mask * (waves[0:1, cols] * (0.4 / K))
        stress_y = 0.3 * speed * north + mask * (waves[1:2, cols] * (0.4 / K))
        rough = mask * 0.2 * jnp.sqrt(stress_x * stress_x + stress_y * stress_y + 0.01)
        onehot = hot(iota((blocks, SW), 0) == p_ref[0:1, cols].astype(I32))
        at = iota((slots // 2, SW), 0) == p_ref[1:2, cols].astype(I32)
        values = jnp.concatenate([jnp.where(at, v, 0.0) for v in (stress_x, stress_y, rough, mask)], axis=0)
        high = values.astype(BF16)
        rest = values - high.astype(F32)
        middle = rest.astype(BF16)
        low = (rest - middle.astype(F32)).astype(BF16)
        total = total + contract(
            jnp.concatenate([onehot] * 3, axis=1), jnp.concatenate([high, middle, low], axis=1), 1, 1
        )
    send_ref[...] = total.reshape(send_ref.shape)


def stresses(tab, got, pts, spectra, wait):
    points = spectra.shape[1]
    blocks = got.shape[0]
    capacity = got.shape[2] // 8
    return pl.pallas_call(
        stress_kernel,
        in_specs=[HERE] * 3 + [AWAY] * 2,
        out_specs=[HERE] * 2,
        out_shape=[
            jax.ShapeDtypeStruct((blocks, 1, 4 * capacity), F32),
            jax.ShapeDtypeStruct((8, points), F32),
        ],
        scratch_shapes=[
            pltpu.VMEM((K, points), BF16),
            pltpu.VMEM((8 * capacity, blocks), BF16),
            pltpu.VMEM((8, points), F32),
            pltpu.SemaphoreType.DMA((points // SW,)),
        ],
        compiler_params=params(BIG),
        cost_estimate=cost(10 * K * points, K * points * 2),
        name="stress",
    )(tab, got, pts, spectra, wait)


def chosen_rows(x, tiles):
    rows = [x[HALF * h + 8 * t : HALF * h + 8 * t + 8] for h in range(2) for t in tiles]
    return jnp.concatenate(rows, axis=0).astype(BF16)


def move_kernel(
    tab_ref, winds_ref, link_ref, got_ref, mean_ref, it_hbm, s_hbm, sb_hbm, sa_hbm, n_hbm,
    out_hbm, token, table, rim, rim_winds, it_ref, s_ref, n_ref, product, natural, south, north, staged, hots, south_y, north_y, flows, sems,
):
    points = link_ref.shape[1]
    parts = points // H + 2
    loads = []
    for g in range(parts):
        to = pl.ds(g * H, H)
        if g == 0:
            source = sb_hbm.at[pl.ds(0, K), :]
        elif g == parts - 1:
            source = sa_hbm.at[pl.ds(0, K), :]
        else:
            source = s_hbm.at[:, pl.ds((g - 1) * H, H)]
        loads.append(pltpu.make_async_copy(source, s_ref.at[:, to], sems.at[g]))
    matrix = pltpu.make_async_copy(it_hbm, it_ref, sems.at[parts])
    products = [
        pltpu.make_async_copy(n_hbm.at[:, pl.ds(g * H, H)], n_ref.at[:, pl.ds(g * H, H)], sems.at[parts + 3 + g])
        for g in range(parts - 2)
    ]
    places = [
        pltpu.make_async_copy(ref.at[pl.ds(K, 16), :], rim.at[k], sems.at[parts + 1 + k])
        for k, ref in enumerate((sb_hbm, sa_hbm))
    ]
    for place in places:
        place.start()

    order = (1, 0, *range(2, parts))

    def start_part(k):
        if k < parts:
            loads[order[k]].start()
            if 0 < order[k] < parts - 1:
                products[order[k] - 1].start()

    start_part(0)
    token[...] = jnp.zeros_like(token)
    width = TW + H

    def build(j, carry):
        mine = pl.ds(pl.multiple_of(j * TW, TW), TW)
        hots[j, 0] = hot(iota((width, TW), 0) == link_ref[2:3, mine] - j * TW)
        hots[j, 1] = hot(iota((width, TW), 0) == link_ref[3:4, mine] - (j * TW + H))
        return carry

    table[...] = got_ref[...].reshape(got_ref.shape[0], got_ref.shape[2]).T.astype(BF16)
    slots = table.shape[0] // 4
    for k in range(2):
        places[k].wait()
        pts = rim[k].astype(F32)
        east, north_, _, _ = winds_at(table[2 * k * slots : (2 * k + 1) * slots, :], pts[0:1], pts[1:2])
        rim_winds[0:1, k * H : (k + 1) * H] = east * pts[2:3]
        rim_winds[1:2, k * H : (k + 1) * H] = north_ * pts[2:3]
        rim_winds[2:3, k * H : (k + 1) * H] = pts[2:3]
    middle = points // TW // 2
    lax.fori_loop(0, middle, build, 0)
    start_part(1)
    matrix.start()
    lax.fori_loop(middle, points // TW, build, 0)
    low = iota((8, 128), 0) < 4

    def fill(i, lanes, mean, kinds):
        at = lane_tile(i)
        if kinds == "sn":
            air, over = winds_ref, lane_tile(i - per)
        else:
            air, over = rim_winds, at if kinds == "s" else lane_tile(i - points // 128)
        pattern = growth_pattern(tab_ref, air[0:1, over], air[1:2, over])
        msk = jnp.broadcast_to(air[2:3, over], (8, 128))
        quota = (0.15 * msk) * jnp.broadcast_to(mean / (1.0 + mean), (8, 128))
        wet = 0.5 * msk
        for m in range(NCH):
            rows = slice(m * CH, (m + 1) * CH)
            s = s_ref[rows, at].astype(F32)
            n = n_ref[rows, lane_tile(i - per)].astype(F32) if kinds == "sn" else product[rows, lanes]
            out = []
            for h in range(2):
                scale = step_scale(m, h)
                power = 1.21 ** (4 * m + 2 * h - NF / 2)
                near = msk - power * quota
                far = msk - (1.21 * power) * quota
                keeps = [near] * 4 + [jnp.where(low, near, far)] + [far] * 4
                for t, keep in enumerate(keeps):
                    tr = slice(8 * t, 8 * t + 8)
                    k = slice(HALF * h + 8 * t, HALF * h + 8 * t + 8)
                    grow = jnp.maximum(scale * pattern[tr] - 0.25, 0.0)
                    out.append(s[k] * (keep + grow) + n[k] * wet)
            x = jnp.concatenate(out, axis=0)
            natural[rows, at] = x.astype(BF16)
            picks = slice(m * 2 * PICK, (m + 1) * 2 * PICK)
            if "s" in kinds:
                south[picks, at] = chosen_rows(x, S_TILES)
            if "n" in kinds:
                north[picks, lane_tile(i - H // 128)] = chosen_rows(x, N_TILES)

    per = H // 128

    def fill_part(g, kinds):
        def own(i, carry):
            fill(i, slice(0, 128), mean_ref[0:1, lane_tile(i - per)], kinds)
            return carry

        if kinds == "sn":
            lax.fori_loop(g * per, (g + 1) * per, own, 0)
            return

        def body(q, carry):
            cols = pl.ds(pl.multiple_of(q * TW, TW), TW)
            product[...] = jnp.dot(it_ref[...], s_ref[:, cols], preferred_element_type=F32)
            acc = jnp.zeros((HALF, TW), F32)
            for m in range(NCH):
                s = s_ref[m * CH : (m + 1) * CH, cols].astype(F32)
                acc = acc + (s[:HALF] + s[HALF:])
            mean = jnp.sum(acc, axis=0, keepdims=True) * (1.0 / K)
            for l in range(TW // 128):
                lanes = slice(l * 128, (l + 1) * 128)
                fill(q * (TW // 128) + l, lanes, mean[:, lanes], kinds)
            return carry

        lax.fori_loop(g * (H // TW), (g + 1) * (H // TW), body, 0)

    def wait_part(k):
        loads[order[k]].wait()
        if 0 < order[k] < parts - 1:
            products[order[k] - 1].wait()
        start_part(k + 2)

    def output(j):
        window = pl.ds(pl.multiple_of(j * TW, TW), width)
        south_y[...] = jnp.dot(south[:, window], hots[j, 0], preferred_element_type=F32)
        north_y[...] = jnp.dot(north[:, window], hots[j, 1], preferred_element_type=F32)
        first = j * (TW // 128) + per
        for l in range(TW // 128):
            msk = winds_ref[2:3, lane_tile(first - per + l)]
            flows[l, 0] = tab_ref[2] * msk
            flows[l, 1] = tab_ref[3] * msk
        lane = iota((8, 128), 1)
        count = TW // 128
        for m in range(NCH):
            rows = slice(m * CH, (m + 1) * CH)
            near = [natural[rows, lane_tile(first + o - 1)].astype(F32) for o in range(count + 2)]
            ys = south_y[m * 2 * PICK : (m + 1) * 2 * PICK, :]
            yn = north_y[m * 2 * PICK : (m + 1) * 2 * PICK, :]
            out = [[] for _ in range(count)]
            for h in range(2):
                shrink = 1.1 ** (-(4 * m + 2 * h))
                for t in range(9):
                    at = slice(HALF * h + 8 * t, HALF * h + 8 * t + 8)
                    tr = slice(8 * t, 8 * t + 8)
                    kind = west_kind(t)
                    tile = [n[at] for n in near]
                    if kind != "east":
                        ahead = [pltpu.roll(x, 1, 1) for x in tile[:-1]]
                    if kind != "west":
                        behind = [pltpu.roll(x, 127, 1) for x in tile[1:]]
                    for l in range(count):
                        c = tile[l + 1]
                        if kind != "east":
                            x = west = jnp.where(lane == 0, ahead[l], ahead[l + 1])
                        if kind != "west":
                            x = east = jnp.where(lane == 127, behind[l + 1], behind[l])
                        if kind == "both":
                            x = jnp.where(tab_ref[5, tr] > 0, west, east)
                        lanes = slice(l * 128, (l + 1) * 128)
                        if t in S_TILES:
                            k = PICK * h + 8 * S_TILES.index(t)
                            y = ys[k : k + 8, lanes]
                        if t in N_TILES:
                            k = PICK * h + 8 * N_TILES.index(t)
                            z = yn[k : k + 8, lanes]
                            y = jnp.where(tab_ref[6, tr] > 0, y, z) if t in S_TILES else z
                        flow = flows[l, 0, tr] * x + flows[l, 1, tr] * y - tab_ref[4, tr] * c
                        out[l].append(c + shrink * flow)
            for l in range(count):
                staged[rows, lane_tile(j * count + l)] = jnp.concatenate(out[l], axis=0).astype(BF16)

    def stores(j):
        at = columns(j)
        return pltpu.make_async_copy(staged.at[:, at], out_hbm.at[:, at], sems.at[2 * parts + 1 + j])

    pair = H // TW
    wait_part(0)
    fill_part(1, "sn")
    wait_part(1)
    matrix.wait()
    fill_part(0, "s")
    for g in range(2, parts):
        wait_part(g)
        fill_part(g, "n" if g == parts - 1 else "sn")
        lax.fori_loop((g - 2) * pair, (g - 1) * pair, lambda j, c: (output(j), stores(j).start(), c)[2], 0)
    for j in range(points // TW):
        stores(j).wait()


def move(tab, winds, links, got, mean, interact, spectra, before, after, nonlinear):
    points = links.shape[1]
    extended = points + 2 * H
    return pl.pallas_call(
        move_kernel,
        in_specs=[HERE] * 5 + [AWAY] * 5,
        out_specs=[AWAY, HERE],
        out_shape=[jax.ShapeDtypeStruct((K, points), BF16), jax.ShapeDtypeStruct((8, 128), F32)],
        scratch_shapes=[
            pltpu.VMEM((got.shape[2], got.shape[0]), BF16),
            pltpu.VMEM((2, 16, H), BF16),
            pltpu.VMEM((8, 2 * H), F32),
            pltpu.VMEM((K, K), BF16),
            pltpu.VMEM((K, extended), BF16),
            pltpu.VMEM((K, points), BF16),
            pltpu.VMEM((K, TW), F32),
            pltpu.VMEM((K, extended), BF16),
            pltpu.VMEM((18 * PICK, points + H), BF16),
            pltpu.VMEM((18 * PICK, points + H), BF16),
            pltpu.VMEM((K, points), BF16),
            pltpu.VMEM((points // TW, 2, TW + H, TW), BF16),
            pltpu.VMEM((18 * PICK, TW), F32),
            pltpu.VMEM((18 * PICK, TW), F32),
            pltpu.VMEM((TW // 128, 2, HALF, 128), F32),
            pltpu.SemaphoreType.DMA((2 * (points // H + 2) + 1 + points // TW,)),
        ],
        compiler_params=params(BIG),
        cost_estimate=cost(2 * 2 * 18 * PICK * (TW + H) * points + 2 * K * K * extended, K * points * 8),
        name="move",
    )(tab, winds, links, got, mean, interact, spectra, before, after, nonlinear)


def cell_kernel(got_ref, push_ref, pusht_ref, air_ref, wait_ref, wind_ref, rough_ref, left, right):
    capacity, blocks = pusht_ref.shape
    lat_dev = air_ref.shape[1]
    values = got_ref[...].reshape(blocks, 4 * capacity).T
    high = values.astype(BF16).astype(F32)
    low = values - high
    for r in range(capacity):
        cols = slice(r * blocks, (r + 1) * blocks)
        at_row = iota((lat_dev, blocks), 0) == (pusht_ref[r : r + 1, :] >> 7)
        for part, source in enumerate((high, low)):
            rows = [
                jnp.where(at_row, source[c * capacity + r : c * capacity + r + 1, :], 0.0) for c in range(4)
            ]
            left[part * 4 * lat_dev : (part + 1) * 4 * lat_dev, cols] = jnp.concatenate(rows, axis=0).astype(BF16)
        right[cols, :] = hot(iota((blocks, 128), 1) == (push_ref[:, r : r + 1] & 127))
    sums = jnp.dot(left[...], right[...], preferred_element_type=F32)
    sums = sums[: 4 * lat_dev] + sums[4 * lat_dev :]
    sx, sy, rough, share = (sums[c * lat_dev : (c + 1) * lat_dev] for c in range(4))
    count = jnp.maximum(share, 1.0)
    wind_ref[0] = air_ref[0] - 0.5 * (sx / count)
    wind_ref[1] = air_ref[1] - 0.5 * (sy / count)
    rough_ref[...] = rough / count


def cells(got, push, pusht, air_state, wait):
    capacity, blocks = pusht.shape
    lat_dev = air_state.shape[1]
    return pl.pallas_call(
        cell_kernel,
        in_specs=[HERE] * 4 + [AWAY],
        out_specs=[HERE] * 2,
        out_shape=[
            jax.ShapeDtypeStruct(air_state.shape, F32),
            jax.ShapeDtypeStruct(air_state.shape[1:], F32),
        ],
        scratch_shapes=[
            pltpu.VMEM((8 * lat_dev, capacity * blocks), BF16),
            pltpu.VMEM((capacity * blocks, 128), BF16),
        ],
        compiler_params=params(BIG),
        cost_estimate=cost(2 * 8 * lat_dev * 128 * capacity * blocks, 400000),
        name="cells",
    )(got, push, pusht, air_state, wait)


def chain(axis, step):
    peers = lax.axis_size(axis)
    pairs = [(i, i + 1) for i in range(peers - 1)]
    return pairs if step > 0 else [(j, i) for i, j in pairs]


def shards(spectra, interact, sea_mask, sea_tile, push_list, neighbors, air_wind, diffusion):
    both = ("wave", "atm")
    tab = jnp.asarray(row_tables())
    lat_total = air_wind.shape[1] * lax.axis_size("atm")
    points = spectra.shape[1]
    push = push_list[0]

    pack = jnp.concatenate([air_wind, diffusion[None]], axis=0)
    above = lax.ppermute(pack[:, -8:], "atm", chain("atm", 1))
    below = lax.ppermute(pack[:, :8], "atm", chain("atm", -1))
    mid = jnp.concatenate([above, pack, below], axis=1)
    pts, pusht, to_prev, to_next = prepare(jnp.stack([sea_tile, sea_mask]), push, spectra)
    mid, pts, pusht, to_prev, to_next = lax.optimization_barrier((mid, pts, pusht, to_prev, to_next))
    left = lax.ppermute(mid, "wave", chain("wave", 1))
    right = lax.ppermute(mid, "wave", chain("wave", -1))


    air_state, outgoing = air(lat_total, mid, left, right, pusht)
    outgoing, to_prev, to_next = lax.optimization_barrier((outgoing, to_prev, to_next))
    arrived = lax.all_to_all(outgoing, both, split_axis=0, concat_axis=0, tiled=True)
    before = lax.ppermute(to_next, both, chain(both, 1))
    after = lax.ppermute(to_prev, both, chain(both, -1))
    nonlinear, mean = interactions(interact, [spectra], points, outgoing, "interact_own")
    outbound, winds = stresses(tab, arrived, pts, spectra, mean)
    inbound = lax.all_to_all(outbound, both, split_axis=0, concat_axis=0, tiled=True)
    wave_spectra, token = move(tab, winds, neighbors, arrived, mean, interact, spectra, before, after, nonlinear)
    surface_wind, roughness = cells(inbound, push, pusht, air_state, token)
    return (wave_spectra, surface_wind, roughness)


def solution(mesh):
    placed = (
        P(None, ("wave", "atm")),
        P(),
        P(("wave", "atm")),
        P(("wave", "atm")),
        P(("wave", "atm"), None, None),
        P(None, ("wave", "atm")),
        P(None, "atm", "wave"),
        P("atm", "wave"),
    )
    return jax.shard_map(
        shards,
        mesh=mesh,
        in_specs=placed,
        out_specs=(P(None, ("wave", "atm")), P(None, "atm", "wave"), P("atm", "wave")),
        check_vma=False,
    )
```
